256 devices in a mesh: tm: 8 (over y, core), space: 32 (over x, z).
Axes of the slice: x: 4, y: 4, z: 8, core: 2. Of those that a mesh axis runs over, the one named last changes fastest.
Arguments:
- snapshots: float32 [2048, 128, 1024], P('space', None, 'tm'), may hold values from -6 to 6
- land_mask: int32 [2048, 128], P('space'), may hold values 0 or 1
- taps_rows: float32 [6], replicated, may hold values from -2.5 to 2.5
- taps_cols: float32 [6], replicated, may hold values from -2.5 to 2.5
- probes: float32 [1024, 64, 128], P('space'), may hold values from -6 to 6
Outputs:
- basis: float32 [1024, 64, 128], P('space', None, 'tm')
- coefficients: float32 [128, 128], P('tm')
The draws below stay inside these ranges and needn't reach their ends.
All inputs are finite; a program needn't handle non-finite values. No bound on the sum of `land_mask` on one device may be relied on, other than what follows from the above.
Results may differ from the reference program's by a relative error of at most 0.00028.
Values sent between devices are 32-bit elements; how exact they have to be, the bound alone decides.
A program may use at most 64 MiB of HBM per device.

```python
import jax
import jax.numpy as jnp
from jax import lax

CY = 128
COLS = 128
NPROBE = 128
SIGN_STEPS = 8
NX = 2048
SNAP = 1024
N_TM = 8


def with_ends(values, stream_key, smallest, top_value):
    index_at = [jax.random.randint(jax.random.fold_in(stream_key, axis), (), 0, length) for axis, length in enumerate(values.shape)]
    main_axis = values.shape.index(max(values.shape))
    next_to = index_at[:main_axis] + [(index_at[main_axis] + 1) % values.shape[main_axis]] + index_at[main_axis + 1:]
    return values.at[tuple(index_at)].set(smallest).at[tuple(next_to)].set(top_value)


def level_of(rng, extent, split, smallest, top_value):
    gain = 1.0
    for dim, shards_of in split:
        steps = jax.random.uniform(jax.random.fold_in(jax.random.fold_in(rng, 6), dim), (shards_of,), jnp.float32, smallest / len(split), top_value / len(split))
        gain = gain * jnp.repeat(jnp.exp(steps), extent[dim] // shards_of).reshape((-1,) + (1,) * (len(extent) - 1 - dim))
    return gain


def noise(stream_key, extent, spread, limit, split=(), held_as=jnp.bfloat16):
    drawn = spread * jax.random.normal(stream_key, extent, jnp.float32)
    if split:
        drawn = drawn * level_of(stream_key, extent, split, -0.22, 0.18)
    return jnp.clip(drawn, -limit, limit).astype(held_as)


def setup_inputs(seed: int = 0) -> dict:
    splits = jax.random.split(jax.random.key(seed), 6)
    return {
        "snapshots": noise(splits[0], (NX, CY, SNAP), 1.0, 6.0, ((0, 32), (2, 8)), jnp.float32),
        "land_mask": with_ends((jax.random.randint(splits[1], (NX, CY), 0, 4) < 3).astype(jnp.int32), jax.random.fold_in(splits[1], 1), 0, 1),
        "taps_rows": noise(splits[2], (6,), 0.5, 2.5, (), jnp.float32),
        "taps_cols": noise(splits[3], (6,), 0.5, 2.5, (), jnp.float32),
        "probes": noise(splits[4], (NX // 2, CY // 2, NPROBE), 1.0, 6.0, ((0, 32),), jnp.float32),
    }


exact_dot = lax.Precision.HIGHEST

def filter_block(block, land_mask, taps_rows, taps_cols):
    ocean_field = block * land_mask.astype(jnp.float32)[:, :, None]
    padded = jnp.pad(ocean_field, ((0, 0), (2, 4), (0, 0)))
    narrowed = taps_cols[0] * padded[:, 0:CY:2, :]
    for tap_index in range(1, 6):
        narrowed = narrowed + taps_cols[tap_index] * padded[:, tap_index:tap_index + CY:2, :]
    padded_rows = jnp.pad(narrowed, ((2, 4), (0, 0), (0, 0)))
    filtered = taps_rows[0] * padded_rows[0:NX:2]
    for tap_index in range(1, 6):
        filtered = filtered + taps_rows[tap_index] * padded_rows[tap_index:tap_index + NX:2]
    return filtered.reshape(NX // 2 * (CY // 2), COLS)

def merge_level(paired):
    gram_total = jnp.einsum('gra,grb->gab', paired, paired, precision=exact_dot)
    order_size = gram_total.shape[-1]
    identity = jnp.eye(order_size, dtype=jnp.float32)
    mean_eig = lax.optimization_barrier(jnp.sum(gram_total * identity, axis=(1, 2))) / order_size
    shifted = gram_total - mean_eig[:, None, None] * identity
    norm_scale = jnp.sqrt(lax.optimization_barrier(jnp.sum(shifted * shifted, axis=(1, 2))) + 1e-06)
    sign_iter = shifted / norm_scale[:, None, None]
    for sweep_index in range(SIGN_STEPS):
        square = jnp.einsum('gab,gbc->gac', sign_iter, sign_iter, precision=exact_dot)
        sign_iter = 1.5 * sign_iter - 0.5 * jnp.einsum('gab,gbc->gac', sign_iter, square, precision=exact_dot)
    projector = 0.5 * (identity + sign_iter)
    half_order = order_size // 2
    combine = projector[:, :, :half_order] + projector[:, :, half_order:]
    return jnp.einsum('gra,gab->grb', paired, combine, precision=exact_dot)

def reference(snapshots, land_mask, taps_rows, taps_cols, probes):
    stacked = snapshots.reshape(NX, CY, N_TM, COLS).transpose(2, 0, 1, 3)

    def filter_one(block):
        return filter_block(block, land_mask, taps_rows, taps_cols)
    blocks = lax.map(filter_one, stacked)
    for level_index in range(N_TM.bit_length() - 1):
        blocks = merge_level(jnp.concatenate([blocks[0::2], blocks[1::2]], axis=2))
    merged = blocks[0]
    flat_probes = probes.reshape(NX // 2 * (CY // 2), NPROBE)
    coefficients = jnp.einsum('rs,rp->sp', merged, flat_probes, precision=exact_dot)
    return (merged.reshape(NX // 2, CY // 2, COLS), coefficients)
```

```python
import functools

import jax
import jax.numpy as jnp
from jax import lax
from jax.experimental import pallas as pl
from jax.experimental.pallas import tpu as pltpu
from jax.sharding import PartitionSpec as P

SIGN_STEPS = 8
NX_CHIPS, NZ_CHIPS = 4, 8
MESH = pl.DeviceIdType.MESH

exact_dot = lax.Precision.HIGHEST


def padded_2(x, sides, width):
    for axis, dim in sides:
        size, length = (lax.axis_size(axis), x.shape[dim])
        up = [(i, (i + 1) % size) for i in range(size - 1)]
        down = [(j, i) for i, j in up]
        last = lax.slice_in_dim(x, length - width, length, axis=dim)
        initial = lax.slice_in_dim(x, 0, width, axis=dim)
        before = lax.ppermute(last, axis, up)
        after = lax.ppermute(initial, axis, down)
        x = jnp.concatenate([before, x, after], axis=dim)
    return x


def partner(block, axis, distance):
    count = lax.axis_size(axis)
    route = []
    for low in range(count):
        high = low | 1 << distance
        if high != low and high < count:
            route += [(low, high), (high, low)]
    return lax.ppermute(block, axis, route)


def band_matrix(tap_values, out_count, in_width, shift_by):
    row_ids = lax.broadcasted_iota(jnp.int32, (out_count, in_width), 0)
    col_ids = lax.broadcasted_iota(jnp.int32, (out_count, in_width), 1)
    tap_offset = col_ids - 2 * row_ids - shift_by
    band_table = jnp.zeros((out_count, in_width), jnp.float32)
    for tap_index in range(6):
        band_table = band_table + jnp.where(tap_offset == tap_index, tap_values[tap_index], 0.0)
    return band_table


def rows_at(start, size):
    return pl.ds(pl.multiple_of(start, 8), size)


def sum_kernel(part, out, zbuf, xbuf, send, recv):
    t = lax.axis_index("tm")
    s = lax.axis_index("space")
    core = t % 2
    x, z = s // NZ_CHIPS, s % NZ_CHIPS
    rows = part.shape[0]
    half = rows // 2
    piece = half // NZ_CHIPS

    def other(d_z=0, d_x=0, flip=False):
        tt = t + 1 - 2 * core if flip else t
        return {
            "tm": tt,
            "space": ((x + d_x) % NX_CHIPS) * NZ_CHIPS + (z + d_z) % NZ_CHIPS,
        }

    barrier = pltpu.get_barrier_semaphore()
    peers = [other(d_z=d) for d in range(1, NZ_CHIPS)]
    peers += [other(d_x=d) for d in range(1, NX_CHIPS)] + [other(flip=True)]
    for peer in peers:
        pl.semaphore_signal(barrier, inc=1, device_id=peer, device_id_type=MESH)
    pl.semaphore_wait(barrier, len(peers))

    def copy(src, dst, index, to):
        return pltpu.make_async_remote_copy(
            src_ref=src,
            dst_ref=dst,
            send_sem=send.at[index],
            recv_sem=recv.at[index],
            device_id=to,
            device_id_type=MESH,
        )

    mine = core * half
    copies = []
    for d in range(1, NZ_CHIPS):
        to = (z + d) % NZ_CHIPS
        c = copy(part.at[rows_at(mine + to * piece, piece)], zbuf.at[d - 1], d - 1, other(d_z=d))
        c.start()
        copies.append(c)
    total = part[rows_at(mine + z * piece, piece), :]
    for c in copies:
        c.wait()
    for d in range(1, NZ_CHIPS):
        total = total + zbuf[d - 1]
    xbuf[x] = total
    copies = []
    for d in range(1, NX_CHIPS):
        c = copy(xbuf.at[x], xbuf.at[x], 6 + d, other(d_x=d))
        c.start()
        copies.append(c)
    for d in range(1, NX_CHIPS):
        copies[d - 1].wait_send()
        came = (x + NX_CHIPS - d) % NX_CHIPS
        copy(xbuf.at[came], xbuf.at[came], 6 + d, other(d_x=d)).wait_recv()
    out[rows_at(mine + z * piece, piece), :] = (xbuf[0] + xbuf[1]) + (xbuf[2] + xbuf[3])
    copies = []
    own = out.at[rows_at(mine + z * piece, piece)]
    for d in range(1, NZ_CHIPS):
        c = copy(own, own, 9 + d, other(d_z=d))
        c.start()
        copies.append(c)
    for d in range(1, NZ_CHIPS):
        copies[d - 1].wait_send()
        came = out.at[rows_at(mine + ((z + NZ_CHIPS - d) % NZ_CHIPS) * piece, piece)]
        copy(came, came, 9 + d, other(d_z=d)).wait_recv()
    ours = out.at[rows_at(mine, half)]
    theirs = out.at[rows_at((1 - core) * half, half)]
    c = copy(ours, ours, 17, other(flip=True))
    c.start()
    c.wait_send()
    copy(theirs, theirs, 17, other(flip=True)).wait_recv()


def plane_sum(part, collective_id):
    rows, cols = part.shape
    piece = rows // 2 // NZ_CHIPS
    return pl.pallas_call(
        sum_kernel,
        out_shape=jax.ShapeDtypeStruct(part.shape, part.dtype),
        in_specs=[pl.BlockSpec(memory_space=pltpu.VMEM)],
        out_specs=pl.BlockSpec(memory_space=pltpu.VMEM),
        scratch_shapes=[
            pltpu.VMEM((NZ_CHIPS - 1, piece, cols), jnp.float32),
            pltpu.VMEM((NX_CHIPS, piece, cols), jnp.float32),
            pltpu.SemaphoreType.DMA((18,)),
            pltpu.SemaphoreType.DMA((18,)),
        ],
        compiler_params=pltpu.CompilerParams(collective_id=collective_id, has_side_effects=True),
        name="plane_sum",
    )(part)


def merge_level(paired):
    half_order = paired.shape[2] // 2
    partial_gram = jnp.einsum("gra,grb->gab", paired, paired, precision=exact_dot)[0]
    stacked = jnp.concatenate(
        [partial_gram[:half_order, :half_order], partial_gram[:half_order, half_order:], partial_gram[half_order:, half_order:]]
    )
    stacked = plane_sum(stacked, 1)
    low, cross, high = jnp.split(stacked, 3)
    gram_total = jnp.concatenate(
        [jnp.concatenate([low, cross], axis=1), jnp.concatenate([cross.T, high], axis=1)]
    )[None]
    order_size = gram_total.shape[-1]
    identity = jnp.eye(order_size, dtype=jnp.float32)
    mean_eig = jnp.sum(gram_total * identity, axis=(1, 2)) / order_size
    shifted = gram_total - mean_eig[:, None, None] * identity
    norm_scale = jnp.sqrt(jnp.sum(shifted * shifted, axis=(1, 2)) + 1e-06)
    sign_iter = shifted / norm_scale[:, None, None]
    for sweep_index in range(SIGN_STEPS):
        square = jnp.einsum("gab,gbc->gac", sign_iter, sign_iter, precision=exact_dot)
        sign_iter = 1.5 * sign_iter - 0.5 * jnp.einsum(
            "gab,gbc->gac", sign_iter, square, precision=exact_dot
        )
    projector = 0.5 * (identity + sign_iter)
    combine = projector[:, :, :half_order] + projector[:, :, half_order:]
    return jnp.einsum("gra,gab->grb", paired, combine, precision=exact_dot)


def local(snapshots, land_mask, taps_rows, taps_cols, probes):
    rows_dev, cell_cols, columns = snapshots.shape
    ocean_field = snapshots * land_mask.astype(jnp.float32)[:, :, None]
    across = band_matrix(taps_cols, cell_cols // 2, cell_cols, -2)
    narrowed = jnp.einsum("jy,xys->xjs", across, ocean_field, precision=exact_dot)
    padded = padded_2(narrowed, (("space", 0),), 3)
    row_filter = band_matrix(taps_rows, rows_dev // 2, rows_dev + 6, 1)
    filtered = jnp.einsum("ip,pjs->ijs", row_filter, padded, precision=exact_dot)
    cell_rows = rows_dev // 2 * (cell_cols // 2)
    factor = filtered.reshape(cell_rows, columns)
    flat_probes = probes.reshape(cell_rows, probes.shape[2])
    levels = lax.axis_size("tm").bit_length() - 1
    position = lax.axis_index("tm")
    merged = factor
    for level_index in range(levels):
        partner_fac = partner(merged, "tm", level_index)
        is_upper = position >> level_index & 1 == 1
        lower_part = jnp.where(is_upper, partner_fac, merged)
        upper_part = jnp.where(is_upper, merged, partner_fac)
        merged = merge_level(jnp.concatenate([lower_part, upper_part], axis=1)[None])
        merged = merged[0]
    width_dev = columns // lax.axis_size("tm")
    col_start = position * width_dev
    partial_coef = jnp.einsum("rs,rp->sp", merged, flat_probes, precision=exact_dot)
    coefficients = plane_sum(partial_coef, 2)
    basis_own = lax.dynamic_slice_in_dim(merged, col_start, width_dev, 1)
    coef_own = lax.dynamic_slice_in_dim(coefficients, col_start, width_dev, 0)
    return (basis_own.reshape(rows_dev // 2, cell_cols // 2, width_dev), coef_own)


def solution(mesh):
    placed = (P("space", None, "tm"), P("space", None), P(), P(), P("space", None, None))
    return jax.shard_map(
        local,
        mesh=mesh,
        in_specs=placed,
        out_specs=(P("space", None, "tm"), P("tm", None)),
        check_vma=False,
    )
```

```python
import functools

import jax
import jax.numpy as jnp
from jax import lax
from jax.experimental import pallas as pl
from jax.experimental.pallas import tpu as pltpu
from jax.sharding import PartitionSpec as P

SIGN_STEPS = 8
NX_CHIPS, NY_CHIPS, NZ_CHIPS = 4, 4, 8
COLS = 128
FIRST_ROWS, SECOND_ROWS = 3 * COLS, 10 * COLS
MESH = pl.DeviceIdType.MESH

exact_dot = lax.Precision.HIGHEST


def padded_2(x, sides, width):
    for axis, dim in sides:
        size, length = (lax.axis_size(axis), x.shape[dim])
        up = [(i, (i + 1) % size) for i in range(size - 1)]
        down = [(j, i) for i, j in up]
        last = lax.slice_in_dim(x, length - width, length, axis=dim)
        initial = lax.slice_in_dim(x, 0, width, axis=dim)
        before = lax.ppermute(last, axis, up)
        after = lax.ppermute(initial, axis, down)
        x = jnp.concatenate([before, x, after], axis=dim)
    return x


def band_matrix(tap_values, out_count, in_width, shift_by):
    row_ids = lax.broadcasted_iota(jnp.int32, (out_count, in_width), 0)
    col_ids = lax.broadcasted_iota(jnp.int32, (out_count, in_width), 1)
    tap_offset = col_ids - 2 * row_ids - shift_by
    band_table = jnp.zeros((out_count, in_width), jnp.float32)
    for tap_index in range(6):
        band_table = band_table + jnp.where(tap_offset == tap_index, tap_values[tap_index], 0.0)
    return band_table


def rows_at(start, size):
    return pl.ds(pl.multiple_of(start, 8), size)


NN = (((1,), (0,)), ((), ()))
TN = (((0,), (0,)), ((), ()))


def halves(a):
    high = a.astype(jnp.bfloat16)
    return high, (a - high.astype(jnp.float32)).astype(jnp.bfloat16)


def dot(a, b, dims):
    return lax.dot_general(a, b, dims, preferred_element_type=jnp.float32)


def dot3(a, b, dims=NN):
    (a_high, a_low), (b_high, b_low) = a, b
    return dot(a_high, b_high, dims) + (dot(a_high, b_low, dims) + dot(a_low, b_high, dims))


def mul(a, b, dims=NN):
    return dot3(halves(a), halves(b), dims)


def block_2x2(low, cross, high):
    return jnp.concatenate(
        [jnp.concatenate([low, cross], axis=1), jnp.concatenate([cross.T, high], axis=1)], axis=0
    )


def start_sign(gram, y_ref):
    order = gram.shape[0]
    identity = lax.broadcasted_iota(jnp.int32, gram.shape, 0) == lax.broadcasted_iota(jnp.int32, gram.shape, 1)
    mean_eig = jnp.sum(jnp.where(identity, gram, 0.0), keepdims=True) / order
    shifted = gram - jnp.where(identity, mean_eig, 0.0)
    y_ref[...] = shifted / jnp.sqrt(jnp.sum(shifted * shifted, keepdims=True) + 1e-06)


def sign_step(y_ref):
    y = y_ref[...]
    y_halves = halves(y)
    square = dot3(y_halves, y_halves)
    y_ref[...] = 1.5 * y - 0.5 * dot3(y_halves, halves(square))


def combine_of(y_ref):
    y = y_ref[...]
    order = y.shape[0]
    row = lax.broadcasted_iota(jnp.int32, (order, order // 2), 0)
    col = lax.broadcasted_iota(jnp.int32, (order, order // 2), 1)
    ones = jnp.where((row == col) | (row == col + order // 2), 0.5, 0.0)
    return ones + 0.5 * (y[:, : order // 2] + y[:, order // 2 :])


def run_signs(*refs):
    def body(step, carry):
        for ref in refs:
            sign_step(ref)
        return carry

    lax.fori_loop(0, SIGN_STEPS, body, 0)


def merge_kernel(factor, probes, pieces, coef, pair, cat_high, cat_low, gram, part1, gath1, cbuf1, zbuf1, xbuf1,
                 quarter, rows4, diag, part2, gath2, cbuf2, zbuf2, xbuf2, ybuf2, sign, probe_rows, turned, coef_all,
                 send, recv, local_sem):
    t = lax.axis_index("tm")
    s = lax.axis_index("space")
    y, core = t // 2, t % 2
    x, z = s // NZ_CHIPS, s % NZ_CHIPS
    half = factor.shape[0] // 2
    own_rows = half // NY_CHIPS

    def at(d_z=0, d_x=0, d_y=0, flip=0):
        c = (core + flip) % 2
        return {
            "tm": ((y + d_y) % NY_CHIPS) * 2 + c,
            "space": ((x + d_x) % NX_CHIPS) * NZ_CHIPS + (z + d_z) % NZ_CHIPS,
        }

    z_offsets = range(1, NZ_CHIPS)
    x_offsets = range(1, NX_CHIPS)
    y_offsets = range(1, NY_CHIPS)
    barrier = pltpu.get_barrier_semaphore()
    peers = [at(d_z=d) for d in z_offsets] + [at(d_x=d) for d in x_offsets]
    peers += [at(d_y=d, flip=f) for f in range(2) for d in range(NY_CHIPS) if d or f]
    for peer in peers:
        pl.semaphore_signal(barrier, inc=1, device_id=peer, device_id_type=MESH)

    count = [0]
    unsent = []

    def push(src, dst, to, landed):
        index = count[0]
        count[0] += 1

        def make(a, b):
            return pltpu.make_async_remote_copy(
                src_ref=a, dst_ref=b, send_sem=send.at[index], recv_sem=recv.at[index], device_id=to, device_id_type=MESH
            )

        out = make(src, dst)
        out.start()
        unsent.append(out)
        return make(landed, landed)

    def arrive(copies):
        for c in copies:
            c.wait_recv()

    take_probes = pltpu.make_async_copy(
        probes.at[rows_at(core * half + y * own_rows, own_rows)], probe_rows, local_sem.at[0]
    )
    take_probes.start()
    take_own = pltpu.make_async_copy(factor.at[rows_at(core * half, half)], pair.at[core], local_sem.at[1])
    take_own.start()
    pl.semaphore_wait(barrier, len(peers))
    arrive([push(factor.at[rows_at((1 - core) * half, half)], pair.at[core], at(flip=1), pair.at[1 - core])])
    take_own.wait()

    def all_sum(part, gath, cbuf, zbuf, xbuf, ybuf):
        rows = part.shape[0] // 2
        piece = rows // NZ_CHIPS
        mine = core * rows
        arrive([push(part.at[rows_at((1 - core) * rows, rows)], cbuf, at(flip=1), cbuf)])
        part[rows_at(mine, rows), :] = part[rows_at(mine, rows), :] + cbuf[...]
        arrive([
            push(part.at[rows_at(mine + (z + d) % NZ_CHIPS * piece, piece)], zbuf.at[d - 1], at(d_z=d), zbuf.at[d - 1])
            for d in z_offsets
        ])
        total = part[rows_at(mine + z * piece, piece), :]
        for d in z_offsets:
            total = total + zbuf[d - 1]
        xbuf[x] = total
        arrive([
            push(xbuf.at[x], xbuf.at[x], at(d_x=d), xbuf.at[(x + NX_CHIPS - d) % NX_CHIPS]) for d in x_offsets
        ])
        total = (xbuf[0] + xbuf[1]) + (xbuf[2] + xbuf[3])
        if ybuf is not None:
            ybuf[y] = total
            arrive([
                push(ybuf.at[y], ybuf.at[y], at(d_y=d), ybuf.at[(y + NY_CHIPS - d) % NY_CHIPS]) for d in y_offsets
            ])
            total = (ybuf[0] + ybuf[1]) + (ybuf[2] + ybuf[3])
        own = gath.at[rows_at(mine + z * piece, piece)]
        gath[rows_at(mine + z * piece, piece), :] = total
        arrive([
            push(own, own, at(d_z=d), gath.at[rows_at(mine + (z + NZ_CHIPS - d) % NZ_CHIPS * piece, piece)])
            for d in z_offsets
        ])
        ours, theirs = gath.at[rows_at(mine, rows)], gath.at[rows_at((1 - core) * rows, rows)]
        arrive([push(ours, ours, at(flip=1), theirs)])

    gram[...] = jnp.zeros_like(gram)

    def add_rows(chunk, carry):
        rows = rows_at(chunk * own_rows, own_rows)
        high, low = halves(jnp.concatenate([pair[0, rows, :], pair[1, rows, :]], axis=1))
        cat_high[rows, :] = high
        cat_low[rows, :] = low
        cross = dot(high, low, TN)
        gram[...] = gram[...] + (dot(high, high, TN) + (cross + cross.T))
        return carry

    lax.fori_loop(0, NY_CHIPS, add_rows, 0)
    part1[:COLS] = gram[:COLS, :COLS]
    part1[COLS : 2 * COLS] = gram[:COLS, COLS:]
    part1[2 * COLS :] = gram[COLS:, COLS:]
    all_sum(part1, gath1, cbuf1, zbuf1, xbuf1, None)
    total = block_2x2(gath1[:COLS], gath1[COLS : 2 * COLS], gath1[2 * COLS :])
    start_sign(total, sign.at[0])
    run_signs(sign.at[0])
    combine = combine_of(sign.at[0])
    combine_halves = halves(combine)

    came = []
    for d in [1, 2, 3, 0]:
        to = (y + d) % NY_CHIPS
        rows = rows_at(to * own_rows, own_rows)
        merged = dot3((cat_high[rows, :], cat_low[rows, :]), combine_halves)
        if d:
            quarter[d - 1] = merged
            came.append(push(quarter.at[d - 1], rows4.at[y], at(d_y=d), rows4.at[(y + NY_CHIPS - d) % NY_CHIPS]))
        else:
            rows4[y] = merged
    diag[y] = mul(combine, mul(total, combine), TN)
    diag_came = [
        push(diag.at[y], diag.at[y], at(d_y=d), diag.at[(y + NY_CHIPS - d) % NY_CHIPS]) for d in y_offsets
    ]
    take_probes.wait()
    arrive(came)

    f4 = [halves(rows4[p]) for p in range(NY_CHIPS)]
    probe_halves = halves(probe_rows[...])
    place = {(0, 1): 0, (2, 3): 1, (0, 2): 2, (0, 3): 3, (1, 2): 4, (1, 3): 5, (0, 4): 6, (1, 4): 7, (2, 4): 8, (3, 4): 9}
    right = f4 + [probe_halves]
    for p in range(NY_CHIPS):
        wide = tuple(jnp.concatenate([right[q][h] for q in range(p + 1, 5)], axis=1) for h in range(2))
        products = dot3(f4[p], wide, TN)
        for q in range(p + 1, 5):
            at_block = place[p, q] * COLS
            part2[at_block : at_block + COLS] = products[:, (q - p - 1) * COLS : (q - p) * COLS]
    all_sum(part2, gath2, cbuf2, zbuf2, xbuf2, ybuf2)
    arrive(diag_came)

    def summed(index):
        return gath2[index * COLS : (index + 1) * COLS]

    gram_low = block_2x2(diag[0], summed(0), diag[1])
    gram_high = block_2x2(diag[2], summed(1), diag[3])
    start_sign(gram_low, sign.at[0])
    start_sign(gram_high, sign.at[1])
    run_signs(sign.at[0], sign.at[1])
    low, high = combine_of(sign.at[0]), combine_of(sign.at[1])
    low_h, high_h = halves(low), halves(high)
    crossing = jnp.concatenate(
        [jnp.concatenate([summed(2), summed(3)], axis=1), jnp.concatenate([summed(4), summed(5)], axis=1)], axis=0
    )
    diag_low = dot3(low_h, halves(dot3(halves(gram_low), low_h)), TN)
    diag_high = dot3(high_h, halves(dot3(halves(gram_high), high_h)), TN)
    cross = dot3(low_h, halves(dot3(halves(crossing), high_h)), TN)

    start_sign(block_2x2(diag_low, cross, diag_high), sign.at[0])
    run_signs(sign.at[0])
    last = combine_of(sign.at[0])
    whole = halves(
        jnp.concatenate([dot3(low_h, halves(last[:COLS])), dot3(high_h, halves(last[COLS:]))], axis=0)
    )
    all4 = tuple(jnp.concatenate([f[h] for f in [halves(rows4[p]) for p in range(NY_CHIPS)]], axis=1) for h in range(2))
    basis = dot3(all4, whole)
    turned[...] = basis.T
    width = COLS // 8
    place_own = core * NY_CHIPS + y
    came = []
    for f in range(2):
        for d in range(NY_CHIPS):
            if d or f:
                to_t = ((y + d) % NY_CHIPS) * 2 + (core + f) % 2
                from_place = ((core + f) % 2) * NY_CHIPS + (y + NY_CHIPS - d) % NY_CHIPS
                came.append(
                    push(turned.at[rows_at(to_t * width, width)], pieces.at[place_own], at(d_y=d, flip=f), pieces.at[from_place])
                )
    pieces[place_own] = turned[rows_at(t * width, width), :]
    coef_all[...] = mul_pair(whole, gath2)
    coef[...] = coef_all[rows_at(t * width, width), :]
    arrive(came)
    for out in unsent:
        out.wait_send()


def mul_pair(whole, gath2):
    return dot3(whole, halves(gath2[6 * COLS :]), TN)


def merge_all(factor, probes):
    rows, cols = factor.shape
    half = rows // 2
    own_rows = half // NY_CHIPS
    f32, vmem = jnp.float32, pltpu.VMEM
    piece1, piece2 = FIRST_ROWS // 16, SECOND_ROWS // 16
    return pl.pallas_call(
        merge_kernel,
        out_shape=(
            jax.ShapeDtypeStruct((8, cols // 8, own_rows), f32),
            jax.ShapeDtypeStruct((cols // 8, cols), f32),
        ),
        in_specs=[pl.BlockSpec(memory_space=pltpu.VMEM), pl.BlockSpec(memory_space=pl.ANY)],
        out_specs=(pl.BlockSpec(memory_space=pltpu.VMEM), pl.BlockSpec(memory_space=pltpu.VMEM)),
        scratch_shapes=[
            vmem((2, half, cols), f32),
            vmem((half, 2 * cols), jnp.bfloat16),
            vmem((half, 2 * cols), jnp.bfloat16),
            vmem((2 * cols, 2 * cols), f32),
            vmem((FIRST_ROWS, cols), f32),
            vmem((FIRST_ROWS, cols), f32),
            vmem((FIRST_ROWS // 2, cols), f32),
            vmem((NZ_CHIPS - 1, piece1, cols), f32),
            vmem((NX_CHIPS, piece1, cols), f32),
            vmem((NY_CHIPS - 1, own_rows, cols), f32),
            vmem((NY_CHIPS, own_rows, cols), f32),
            vmem((NY_CHIPS, cols, cols), f32),
            vmem((SECOND_ROWS, cols), f32),
            vmem((SECOND_ROWS, cols), f32),
            vmem((SECOND_ROWS // 2, cols), f32),
            vmem((NZ_CHIPS - 1, piece2, cols), f32),
            vmem((NX_CHIPS, piece2, cols), f32),
            vmem((NY_CHIPS, piece2, cols), f32),
            vmem((2, 2 * cols, 2 * cols), f32),
            vmem((own_rows, cols), f32),
            vmem((cols, own_rows), f32),
            vmem((cols, cols), f32),
            pltpu.SemaphoreType.DMA((64,)),
            pltpu.SemaphoreType.DMA((64,)),
            pltpu.SemaphoreType.DMA((2,)),
        ],
        compiler_params=pltpu.CompilerParams(
            collective_id=1, has_side_effects=True, vmem_limit_bytes=32 << 20
        ),
        name="merge_all",
    )(factor, probes)


def local(snapshots, land_mask, taps_rows, taps_cols, probes):
    rows_dev, cell_cols, columns = snapshots.shape
    ocean_field = snapshots * land_mask.astype(jnp.float32)[:, :, None]
    across = band_matrix(taps_cols, cell_cols // 2, cell_cols, -2)
    narrowed = jnp.einsum("jy,xys->xjs", across, ocean_field, precision=exact_dot)
    padded = padded_2(narrowed, (("space", 0),), 3)
    row_filter = band_matrix(taps_rows, rows_dev // 2, rows_dev + 6, 1)
    filtered = jnp.einsum("ip,pjs->ijs", row_filter, padded, precision=exact_dot)
    cell_rows = rows_dev // 2 * (cell_cols // 2)
    factor = filtered.reshape(cell_rows, columns)
    flat_probes = probes.reshape(cell_rows, probes.shape[2])
    pieces, coef_own = merge_all(factor, flat_probes)
    basis_own = pieces.transpose(0, 2, 1)
    return (basis_own.reshape(rows_dev // 2, cell_cols // 2, columns // 8), coef_own)


def solution(mesh):
    placed = (P("space", None, "tm"), P("space", None), P(), P(), P("space", None, None))
    return jax.shard_map(
        local,
        mesh=mesh,
        in_specs=placed,
        out_specs=(P("space", None, "tm"), P("tm", None)),
        check_vma=False,
    )
```

```python
import functools

import jax
import jax.numpy as jnp
from jax import lax
from jax.experimental import pallas as pl
from jax.experimental.pallas import tpu as pltpu
from jax.sharding import PartitionSpec as P

SIGN_STEPS = 8
NX_CHIPS, NY_CHIPS, NZ_CHIPS = 4, 4, 8
SPACE = NX_CHIPS * NZ_CHIPS
COLS = 128
FIRST_ROWS, SECOND_ROWS = 3 * COLS, 10 * COLS
TAPS, CHUNK, EDGE = 6, 8, 8
MESH = pl.DeviceIdType.MESH

def rows_at(start, size):
    return pl.ds(pl.multiple_of(start, 8), size)


NN = (((1,), (0,)), ((), ()))
TN = (((0,), (0,)), ((), ()))


def halves(a):
    high = a.astype(jnp.bfloat16)
    return high, (a - high.astype(jnp.float32)).astype(jnp.bfloat16)


def dot(a, b, dims):
    return lax.dot_general(a, b, dims, preferred_element_type=jnp.float32)


def dot3(a, b, dims=NN):
    (a_high, a_low), (b_high, b_low) = a, b
    return dot(a_high, b_high, dims) + (dot(a_high, b_low, dims) + dot(a_low, b_high, dims))


def mul(a, b, dims=NN):
    return dot3(halves(a), halves(b), dims)


def block_2x2(low, cross, high):
    return jnp.concatenate(
        [jnp.concatenate([low, cross], axis=1), jnp.concatenate([cross.T, high], axis=1)], axis=0
    )


def start_sign(gram, y_ref):
    order = gram.shape[0]
    identity = lax.broadcasted_iota(jnp.int32, gram.shape, 0) == lax.broadcasted_iota(jnp.int32, gram.shape, 1)
    mean_eig = jnp.sum(jnp.where(identity, gram, 0.0), keepdims=True) / order
    shifted = gram - jnp.where(identity, mean_eig, 0.0)
    y_ref[...] = shifted / jnp.sqrt(jnp.sum(shifted * shifted, keepdims=True) + 1e-06)


def sign_step(y_ref):
    y = y_ref[...]
    y_halves = halves(y)
    square = dot3(y_halves, y_halves)
    y_ref[...] = 1.5 * y - 0.5 * dot3(y_halves, halves(square))


def combine_of(y_ref):
    y = y_ref[...]
    order = y.shape[0]
    row = lax.broadcasted_iota(jnp.int32, (order, order // 2), 0)
    col = lax.broadcasted_iota(jnp.int32, (order, order // 2), 1)
    ones = jnp.where((row == col) | (row == col + order // 2), 0.5, 0.0)
    return ones + 0.5 * (y[:, : order // 2] + y[:, order // 2 :])


def run_signs(*refs):
    def body(step, carry):
        for ref in refs:
            sign_step(ref)
        return carry

    lax.fori_loop(0, SIGN_STEPS, body, 0)


def merge_kernel(snapshots, mask, taps_rows, taps_cols, probes, pieces, coef,
                 field, mask_own, mask_ends, tall, away, pair, cat_high, cat_low, gram, part1, gath1, cbuf1, zbuf1, xbuf1,
                 quarter, rows4, diag, part2, gath2, cbuf2, zbuf2, xbuf2, ybuf2, sign, probe_rows, turned, coef_all,
                 send, recv, local_sem, chunk_sem):
    t = lax.axis_index("tm")
    s = lax.axis_index("space")
    y, core = t // 2, t % 2
    x, z = s // NZ_CHIPS, s % NZ_CHIPS
    rows_dev, cells = snapshots.shape[0], snapshots.shape[1]
    out_rows, out_cells = rows_dev // 2, cells // 2
    half = out_rows * out_cells // 2
    chunks = rows_dev // CHUNK
    own_rows = half // NY_CHIPS

    def at(d_z=0, d_x=0, d_y=0, flip=0):
        c = (core + flip) % 2
        return {
            "tm": ((y + d_y) % NY_CHIPS) * 2 + c,
            "space": ((x + d_x) % NX_CHIPS) * NZ_CHIPS + (z + d_z) % NZ_CHIPS,
        }

    z_offsets = range(1, NZ_CHIPS)
    x_offsets = range(1, NX_CHIPS)
    y_offsets = range(1, NY_CHIPS)
    s_above, s_below = (s + SPACE - 1) % SPACE, (s + 1) % SPACE
    above, below = {"tm": t, "space": s_above}, {"tm": t, "space": s_below}
    barrier = pltpu.get_barrier_semaphore()
    peers = [at(d_z=d) for d in z_offsets] + [at(d_x=d) for d in x_offsets]
    peers += [at(d_y=d, flip=f) for f in range(2) for d in range(NY_CHIPS) if d or f]
    peers += [above, below]
    for peer in peers:
        pl.semaphore_signal(barrier, inc=1, device_id=peer, device_id_type=MESH)

    count = [0]
    unsent = []

    def push(src, dst, to, landed):
        index = count[0]
        count[0] += 1

        def make(a, b):
            return pltpu.make_async_remote_copy(
                src_ref=a, dst_ref=b, send_sem=send.at[index], recv_sem=recv.at[index], device_id=to, device_id_type=MESH
            )

        out = make(src, dst)
        out.start()
        unsent.append(out)
        return make(landed, landed)

    def arrive(copies):
        for c in copies:
            c.wait_recv()

    take_probes = pltpu.make_async_copy(
        probes.at[rows_at(core * half + y * own_rows, own_rows)], probe_rows, local_sem.at[0]
    )
    take_probes.start()
    take_mask = pltpu.make_async_copy(mask, mask_own.at[pl.ds(0, rows_dev)], local_sem.at[1])
    take_mask.start()

    def chunk_copy(k):
        first = (core * k + (1 - core) * (chunks - 1 - k)) * CHUNK
        return pltpu.make_async_copy(
            snapshots.at[pl.ds(first, CHUNK)], field.at[pl.ds(first + 2, CHUNK)], chunk_sem.at[k]
        )

    for k in range(chunks):
        chunk_copy(k).start()
    mask_own[rows_dev:, :] = jnp.zeros((COLS - rows_dev, cells), jnp.int32)
    tall[:, :EDGE] = jnp.zeros((tall.shape[0], EDGE, COLS), jnp.float32)
    tall[:, EDGE + cells :] = jnp.zeros((tall.shape[0], EDGE, COLS), jnp.float32)
    take_mask.wait()
    mask_cols = mask_own[...].astype(jnp.float32).T

    def mask_chunk(k):
        chunk_copy(k).wait()
        first = (core * k + (1 - core) * (chunks - 1 - k)) * CHUNK
        turned_mask = pltpu.roll(mask_cols, (COLS - first) % COLS, axis=1)
        for r in range(CHUNK):
            field[first + 2 + r] = field[first + 2 + r] * turned_mask[:, r : r + 1]

    tr = [taps_rows[k] for k in range(TAPS)]
    tc = [taps_cols[k] for k in range(TAPS)]

    def filter_row(i, slot):
        total = tr[0] * field[2 * i]
        for k in range(1, TAPS):
            total = total + tr[k] * field[2 * i + k]
        tall[slot, EDGE : EDGE + cells] = total
        out = tc[0] * tall[slot, pl.ds(EDGE - 2, out_cells, stride=2), :]
        for k in range(1, TAPS):
            out = out + tc[k] * tall[slot, pl.ds(EDGE - 2 + k, out_cells, stride=2), :]
        return out

    def filter_rows(first, store):
        def body(step, carry):
            for slot in range(tall.shape[0]):
                n = step * tall.shape[0] + slot
                store(n, filter_row(first + n, slot))
            return carry

        lax.fori_loop(0, (out_rows // 2 - 1) // tall.shape[0], body, 0)

    def store_away(n, value):
        away[rows_at((n + core) * out_cells, out_cells), :] = value

    def store_own(n, value):
        pair[core, rows_at((n + 1 - core) * out_cells, out_cells), :] = value

    inner = half - out_cells
    for k in range(chunks // 2 + 1):
        mask_chunk(k)
    pl.semaphore_wait(barrier, len(peers))
    came = [
        push(snapshots.at[pl.ds(rows_dev - 2, 2)], field.at[pl.ds(0, 2)], below, field.at[pl.ds(0, 2)]),
        push(snapshots.at[pl.ds(0, 2)], field.at[pl.ds(rows_dev + 2, 2)], above, field.at[pl.ds(rows_dev + 2, 2)]),
        push(mask.at[pl.ds(rows_dev - 8, 8)], mask_ends.at[pl.ds(0, 8)], below, mask_ends.at[pl.ds(0, 8)]),
        push(mask.at[pl.ds(0, 8)], mask_ends.at[pl.ds(8, 8)], above, mask_ends.at[pl.ds(8, 8)]),
    ]
    filter_rows(1 + (out_rows // 2 - 1) * (1 - core), store_away)
    crossed = [
        push(
            away.at[rows_at(core * out_cells, inner)],
            pair.at[core, rows_at(core * out_cells, inner)],
            at(flip=1),
            pair.at[1 - core, rows_at((1 - core) * out_cells, inner)],
        )
    ]
    for k in range(chunks // 2 + 1, chunks):
        mask_chunk(k)
    filter_rows(1 + (out_rows // 2 - 1) * core, store_own)
    arrive(came)
    ends = mask_ends[...].astype(jnp.float32)
    ends = jnp.concatenate(
        [jnp.where(s > 0, ends[:8], 0.0), jnp.where(s < SPACE - 1, ends[8:], 0.0), jnp.zeros((COLS - 16, cells), jnp.float32)],
        axis=0,
    ).T
    for row, lane in ((0, 6), (1, 7), (rows_dev + 2, 8), (rows_dev + 3, 9)):
        field[row] = field[row] * ends[:, lane : lane + 1]
    last_away = rows_at((out_rows // 2 - 1) * out_cells * (1 - core), out_cells)
    last_own = rows_at((out_rows // 2 - 1) * out_cells * core, out_cells)
    away[last_away, :] = filter_row((out_rows - 1) * (1 - core), 0)
    crossed.append(
        push(away.at[last_away], pair.at[core, last_away], at(flip=1), pair.at[1 - core, last_own])
    )
    pair[core, last_own, :] = filter_row((out_rows - 1) * core, 1)
    arrive(crossed)

    def all_sum(part, gath, cbuf, zbuf, xbuf, ybuf):
        rows = part.shape[0] // 2
        piece = rows // NZ_CHIPS
        mine = core * rows
        arrive([push(part.at[rows_at((1 - core) * rows, rows)], cbuf, at(flip=1), cbuf)])
        part[rows_at(mine, rows), :] = part[rows_at(mine, rows), :] + cbuf[...]
        arrive([
            push(part.at[rows_at(mine + (z + d) % NZ_CHIPS * piece, piece)], zbuf.at[d - 1], at(d_z=d), zbuf.at[d - 1])
            for d in z_offsets
        ])
        total = part[rows_at(mine + z * piece, piece), :]
        for d in z_offsets:
            total = total + zbuf[d - 1]
        xbuf[x] = total
        arrive([
            push(xbuf.at[x], xbuf.at[x], at(d_x=d), xbuf.at[(x + NX_CHIPS - d) % NX_CHIPS]) for d in x_offsets
        ])
        total = (xbuf[0] + xbuf[1]) + (xbuf[2] + xbuf[3])
        if ybuf is not None:
            ybuf[y] = total
            arrive([
                push(ybuf.at[y], ybuf.at[y], at(d_y=d), ybuf.at[(y + NY_CHIPS - d) % NY_CHIPS]) for d in y_offsets
            ])
            total = (ybuf[0] + ybuf[1]) + (ybuf[2] + ybuf[3])
        own = gath.at[rows_at(mine + z * piece, piece)]
        gath[rows_at(mine + z * piece, piece), :] = total
        arrive([
            push(own, own, at(d_z=d), gath.at[rows_at(mine + (z + NZ_CHIPS - d) % NZ_CHIPS * piece, piece)])
            for d in z_offsets
        ])
        ours, theirs = gath.at[rows_at(mine, rows)], gath.at[rows_at((1 - core) * rows, rows)]
        arrive([push(ours, ours, at(flip=1), theirs)])

    gram[...] = jnp.zeros_like(gram)

    def add_rows(chunk, carry):
        rows = rows_at(chunk * own_rows, own_rows)
        high, low = halves(jnp.concatenate([pair[0, rows, :], pair[1, rows, :]], axis=1))
        cat_high[rows, :] = high
        cat_low[rows, :] = low
        cross = dot(high, low, TN)
        gram[...] = gram[...] + (dot(high, high, TN) + (cross + cross.T))
        return carry

    lax.fori_loop(0, NY_CHIPS, add_rows, 0)
    part1[:COLS] = gram[:COLS, :COLS]
    part1[COLS : 2 * COLS] = gram[:COLS, COLS:]
    part1[2 * COLS :] = gram[COLS:, COLS:]
    all_sum(part1, gath1, cbuf1, zbuf1, xbuf1, None)
    total = block_2x2(gath1[:COLS], gath1[COLS : 2 * COLS], gath1[2 * COLS :])
    start_sign(total, sign.at[0])
    run_signs(sign.at[0])
    combine = combine_of(sign.at[0])
    combine_halves = halves(combine)

    came = []
    for d in [1, 2, 3, 0]:
        to = (y + d) % NY_CHIPS
        rows = rows_at(to * own_rows, own_rows)
        merged = dot3((cat_high[rows, :], cat_low[rows, :]), combine_halves)
        if d:
            quarter[d - 1] = merged
            came.append(push(quarter.at[d - 1], rows4.at[y], at(d_y=d), rows4.at[(y + NY_CHIPS - d) % NY_CHIPS]))
        else:
            rows4[y] = merged
    diag[y] = mul(combine, mul(total, combine), TN)
    diag_came = [
        push(diag.at[y], diag.at[y], at(d_y=d), diag.at[(y + NY_CHIPS - d) % NY_CHIPS]) for d in y_offsets
    ]
    take_probes.wait()
    arrive(came)

    f4 = [halves(rows4[p]) for p in range(NY_CHIPS)]
    probe_halves = halves(probe_rows[...])
    place = {(0, 1): 0, (2, 3): 1, (0, 2): 2, (0, 3): 3, (1, 2): 4, (1, 3): 5, (0, 4): 6, (1, 4): 7, (2, 4): 8, (3, 4): 9}
    right = f4 + [probe_halves]
    for p in range(NY_CHIPS):
        wide = tuple(jnp.concatenate([right[q][h] for q in range(p + 1, 5)], axis=1) for h in range(2))
        products = dot3(f4[p], wide, TN)
        for q in range(p + 1, 5):
            at_block = place[p, q] * COLS
            part2[at_block : at_block + COLS] = products[:, (q - p - 1) * COLS : (q - p) * COLS]
    all_sum(part2, gath2, cbuf2, zbuf2, xbuf2, ybuf2)
    arrive(diag_came)

    def summed(index):
        return gath2[index * COLS : (index + 1) * COLS]

    gram_low = block_2x2(diag[0], summed(0), diag[1])
    gram_high = block_2x2(diag[2], summed(1), diag[3])
    start_sign(gram_low, sign.at[0])
    start_sign(gram_high, sign.at[1])
    run_signs(sign.at[0], sign.at[1])
    low, high = combine_of(sign.at[0]), combine_of(sign.at[1])
    low_h, high_h = halves(low), halves(high)
    crossing = jnp.concatenate(
        [jnp.concatenate([summed(2), summed(3)], axis=1), jnp.concatenate([summed(4), summed(5)], axis=1)], axis=0
    )
    diag_low = dot3(low_h, halves(dot3(halves(gram_low), low_h)), TN)
    diag_high = dot3(high_h, halves(dot3(halves(gram_high), high_h)), TN)
    cross = dot3(low_h, halves(dot3(halves(crossing), high_h)), TN)

    start_sign(block_2x2(diag_low, cross, diag_high), sign.at[0])
    run_signs(sign.at[0])
    last = combine_of(sign.at[0])
    whole = halves(
        jnp.concatenate([dot3(low_h, halves(last[:COLS])), dot3(high_h, halves(last[COLS:]))], axis=0)
    )
    all4 = tuple(jnp.concatenate([f[h] for f in [halves(rows4[p]) for p in range(NY_CHIPS)]], axis=1) for h in range(2))
    basis = dot3(all4, whole)
    turned[...] = basis.T
    width = COLS // 8
    place_own = core * NY_CHIPS + y
    came = []
    for f in range(2):
        for d in range(NY_CHIPS):
            if d or f:
                to_t = ((y + d) % NY_CHIPS) * 2 + (core + f) % 2
                from_place = ((core + f) % 2) * NY_CHIPS + (y + NY_CHIPS - d) % NY_CHIPS
                came.append(
                    push(turned.at[rows_at(to_t * width, width)], pieces.at[place_own], at(d_y=d, flip=f), pieces.at[from_place])
                )
    pieces[place_own] = turned[rows_at(t * width, width), :]
    coef_all[...] = mul_pair(whole, gath2)
    coef[...] = coef_all[rows_at(t * width, width), :]
    arrive(came)
    for out in unsent:
        out.wait_send()


def mul_pair(whole, gath2):
    return dot3(whole, halves(gath2[6 * COLS :]), TN)


def merge_all(snapshots, mask, taps_rows, taps_cols, probes):
    rows_dev, cells, cols = snapshots.shape
    rows = rows_dev // 2 * (cells // 2)
    half = rows // 2
    own_rows = half // NY_CHIPS
    f32, vmem = jnp.float32, pltpu.VMEM
    piece1, piece2 = FIRST_ROWS // 16, SECOND_ROWS // 16
    return pl.pallas_call(
        merge_kernel,
        out_shape=(
            jax.ShapeDtypeStruct((8, cols // 8, own_rows), f32),
            jax.ShapeDtypeStruct((cols // 8, cols), f32),
        ),
        in_specs=[pl.BlockSpec(memory_space=pl.ANY)] * 2
        + [pl.BlockSpec(memory_space=pltpu.SMEM)] * 2
        + [pl.BlockSpec(memory_space=pl.ANY)],
        out_specs=(pl.BlockSpec(memory_space=pltpu.VMEM), pl.BlockSpec(memory_space=pltpu.VMEM)),
        scratch_shapes=[
            vmem((rows_dev + 4, cells, cols), f32),
            vmem((COLS, cells), jnp.int32),
            vmem((16, cells), jnp.int32),
            vmem((3, cells + 2 * EDGE, cols), f32),
            vmem((half, cols), f32),
            vmem((2, half, cols), f32),
            vmem((half, 2 * cols), jnp.bfloat16),
            vmem((half, 2 * cols), jnp.bfloat16),
            vmem((2 * cols, 2 * cols), f32),
            vmem((FIRST_ROWS, cols), f32),
            vmem((FIRST_ROWS, cols), f32),
            vmem((FIRST_ROWS // 2, cols), f32),
            vmem((NZ_CHIPS - 1, piece1, cols), f32),
            vmem((NX_CHIPS, piece1, cols), f32),
            vmem((NY_CHIPS - 1, own_rows, cols), f32),
            vmem((NY_CHIPS, own_rows, cols), f32),
            vmem((NY_CHIPS, cols, cols), f32),
            vmem((SECOND_ROWS, cols), f32),
            vmem((SECOND_ROWS, cols), f32),
            vmem((SECOND_ROWS // 2, cols), f32),
            vmem((NZ_CHIPS - 1, piece2, cols), f32),
            vmem((NX_CHIPS, piece2, cols), f32),
            vmem((NY_CHIPS, piece2, cols), f32),
            vmem((2, 2 * cols, 2 * cols), f32),
            vmem((own_rows, cols), f32),
            vmem((cols, own_rows), f32),
            vmem((cols, cols), f32),
            pltpu.SemaphoreType.DMA((64,)),
            pltpu.SemaphoreType.DMA((64,)),
            pltpu.SemaphoreType.DMA((2,)),
            pltpu.SemaphoreType.DMA((rows_dev // CHUNK,)),
        ],
        compiler_params=pltpu.CompilerParams(
            collective_id=1, has_side_effects=True, vmem_limit_bytes=32 << 20
        ),
        name="merge_all",
    )(snapshots, mask, taps_rows, taps_cols, probes)


def local(snapshots, land_mask, taps_rows, taps_cols, probes):
    rows_dev, cell_cols, columns = snapshots.shape
    cell_rows = rows_dev // 2 * (cell_cols // 2)
    flat_probes = probes.reshape(cell_rows, probes.shape[2])
    pieces, coef_own = merge_all(snapshots, land_mask, taps_rows, taps_cols, flat_probes)
    basis_own = pieces.transpose(0, 2, 1)
    return (basis_own.reshape(rows_dev // 2, cell_cols // 2, columns // 8), coef_own)


def solution(mesh):
    placed = (P("space", None, "tm"), P("space", None), P(), P(), P("space", None, None))
    return jax.shard_map(
        local,
        mesh=mesh,
        in_specs=placed,
        out_specs=(P("space", None, "tm"), P("tm", None)),
        check_vma=False,
    )
```

```python
import functools

import jax
import jax.numpy as jnp
from jax import lax
from jax.experimental import pallas as pl
from jax.experimental.pallas import tpu as pltpu
from jax.sharding import PartitionSpec as P

SIGN_STEPS = 8
NX_CHIPS, NY_CHIPS, NZ_CHIPS = 4, 4, 8
SPACE, XY_CHIPS = NX_CHIPS * NZ_CHIPS, NX_CHIPS * NY_CHIPS
COLS = 128
FIRST_ROWS, SECOND_ROWS, LATER_ROWS = 3 * COLS, 2 * COLS, 8 * COLS
TAPS, CHUNK, EDGE = 6, 8, 8
MESH = pl.DeviceIdType.MESH

def rows_at(start, size):
    return pl.ds(pl.multiple_of(start, 8), size)


NN = (((1,), (0,)), ((), ()))
TN = (((0,), (0,)), ((), ()))


def halves(a):
    high = a.astype(jnp.bfloat16)
    return high, (a - high.astype(jnp.float32)).astype(jnp.bfloat16)


def dot(a, b, dims):
    return lax.dot_general(a, b, dims, preferred_element_type=jnp.float32)


def dot3(a, b, dims=NN):
    (a_high, a_low), (b_high, b_low) = a, b
    return dot(a_high, b_high, dims) + (dot(a_high, b_low, dims) + dot(a_low, b_high, dims))


def mul(a, b, dims=NN):
    return dot3(halves(a), halves(b), dims)


def block_2x2(low, cross, high):
    return jnp.concatenate(
        [jnp.concatenate([low, cross], axis=1), jnp.concatenate([cross.T, high], axis=1)], axis=0
    )


def start_sign(gram, y_ref):
    order = gram.shape[0]
    identity = lax.broadcasted_iota(jnp.int32, gram.shape, 0) == lax.broadcasted_iota(jnp.int32, gram.shape, 1)
    mean_eig = jnp.sum(jnp.where(identity, gram, 0.0), keepdims=True) / order
    shifted = gram - jnp.where(identity, mean_eig, 0.0)
    y_ref[...] = shifted / jnp.sqrt(jnp.sum(shifted * shifted, keepdims=True) + 1e-06)


def sign_step(y_ref):
    y = y_ref[...]
    y_halves = halves(y)
    square = dot3(y_halves, y_halves)
    y_ref[...] = 1.5 * y - 0.5 * dot3(y_halves, halves(square))


def combine_of(y_ref):
    y = y_ref[...]
    order = y.shape[0]
    row = lax.broadcasted_iota(jnp.int32, (order, order // 2), 0)
    col = lax.broadcasted_iota(jnp.int32, (order, order // 2), 1)
    ones = jnp.where((row == col) | (row == col + order // 2), 0.5, 0.0)
    return ones + 0.5 * (y[:, : order // 2] + y[:, order // 2 :])


def run_signs(steps, *refs):
    def body(step, carry):
        for ref in refs:
            sign_step(ref)
        return carry

    lax.fori_loop(0, steps, body, 0)


def merge_kernel(snapshots, mask, taps_rows, taps_cols, probes, pieces, coef,
                 row_taps, col_taps, field, mask_own, mask_ends, tall, away, pair, cat_high, cat_low, gram, part1, gath1, cbuf1, zbuf1, xbuf1,
                 quarter, rows4, diag, part2, gath2, cbuf2, rbuf2, zbuf2,
                 part3, gath3, cbuf3, rbuf3, zbuf3, sign, probe_rows, turned, coef_all,
                 send, recv, local_sem, chunk_sem):
    t = lax.axis_index("tm")
    s = lax.axis_index("space")
    y, core = t // 2, t % 2
    x, z = s // NZ_CHIPS, s % NZ_CHIPS
    rows_dev, cells = snapshots.shape[0], snapshots.shape[1]
    out_rows, out_cells = rows_dev // 2, cells // 2
    half = out_rows * out_cells // 2
    chunks = rows_dev // CHUNK
    own_rows = half // NY_CHIPS

    def at(d_z=0, d_x=0, d_y=0, flip=0):
        c = (core + flip) % 2
        return {
            "tm": ((y + d_y) % NY_CHIPS) * 2 + c,
            "space": ((x + d_x) % NX_CHIPS) * NZ_CHIPS + (z + d_z) % NZ_CHIPS,
        }

    z_offsets = range(1, NZ_CHIPS)
    x_offsets = range(1, NX_CHIPS)
    y_offsets = range(1, NY_CHIPS)
    s_above, s_below = (s + SPACE - 1) % SPACE, (s + 1) % SPACE
    above, below = {"tm": t, "space": s_above}, {"tm": t, "space": s_below}
    barrier = pltpu.get_barrier_semaphore()
    xy_offsets = [(a, b) for a in range(NX_CHIPS) for b in range(NY_CHIPS) if a or b]
    peers = [at(d_z=d) for d in z_offsets] + [at(d_x=a, d_y=b) for a, b in xy_offsets]
    peers += [at(d_y=d, flip=1) for d in range(NY_CHIPS)]
    peers += [above, below]
    for peer in peers:
        pl.semaphore_signal(barrier, inc=1, device_id=peer, device_id_type=MESH)

    count = [0]
    unsent = []

    def push(src, dst, to, landed):
        index = count[0]
        count[0] += 1

        def make(a, b):
            return pltpu.make_async_remote_copy(
                src_ref=a, dst_ref=b, send_sem=send.at[index], recv_sem=recv.at[index], device_id=to, device_id_type=MESH
            )

        out = make(src, dst)
        out.start()
        unsent.append(out)
        return make(landed, landed)

    def arrive(copies):
        for c in copies:
            c.wait_recv()

    take_probes = pltpu.make_async_copy(
        probes.at[rows_at(core * half + y * own_rows, own_rows)], probe_rows, local_sem.at[0]
    )
    take_probes.start()
    take_mask = pltpu.make_async_copy(mask, mask_own.at[pl.ds(0, rows_dev)], local_sem.at[1])
    take_mask.start()
    take_taps = [
        pltpu.make_async_copy(taps_rows, row_taps, local_sem.at[2]),
        pltpu.make_async_copy(taps_cols, col_taps, local_sem.at[3]),
    ]
    for taps in take_taps:
        taps.start()

    def chunk_copy(k):
        first = (core * k + (1 - core) * (chunks - 1 - k)) * CHUNK
        return pltpu.make_async_copy(
            snapshots.at[pl.ds(first, CHUNK)], field.at[pl.ds(first + 2, CHUNK)], chunk_sem.at[k]
        )

    for k in range(chunks):
        chunk_copy(k).start()
    mask_own[rows_dev:, :] = jnp.zeros((COLS - rows_dev, cells), jnp.int32)
    tall[:, :EDGE] = jnp.zeros((tall.shape[0], EDGE, COLS), jnp.float32)
    tall[:, EDGE + cells :] = jnp.zeros((tall.shape[0], EDGE, COLS), jnp.float32)
    take_mask.wait()
    mask_cols = mask_own[...].astype(jnp.float32).T

    def mask_chunk(k):
        chunk_copy(k).wait()
        first = (core * k + (1 - core) * (chunks - 1 - k)) * CHUNK
        turned_mask = pltpu.roll(mask_cols, (COLS - first) % COLS, axis=1)
        for r in range(CHUNK):
            field[first + 2 + r] = field[first + 2 + r] * turned_mask[:, r : r + 1]

    for taps in take_taps:
        taps.wait()
    tr = [row_taps[k] for k in range(TAPS)]
    tc = [col_taps[k] for k in range(TAPS)]

    def filter_row(i, slot):
        total = tr[0] * field[2 * i]
        for k in range(1, TAPS):
            total = total + tr[k] * field[2 * i + k]
        tall[slot, EDGE : EDGE + cells] = total
        out = tc[0] * tall[slot, pl.ds(EDGE - 2, out_cells, stride=2), :]
        for k in range(1, TAPS):
            out = out + tc[k] * tall[slot, pl.ds(EDGE - 2 + k, out_cells, stride=2), :]
        return out

    def filter_rows(first, store):
        def body(step, carry):
            for slot in range(tall.shape[0]):
                n = step * tall.shape[0] + slot
                store(n, filter_row(first + n, slot))
            return carry

        lax.fori_loop(0, (out_rows // 2 - 1) // tall.shape[0], body, 0)

    def store_away(n, value):
        away[rows_at((n + core) * out_cells, out_cells), :] = value

    def store_own(n, value):
        pair[core, rows_at((n + 1 - core) * out_cells, out_cells), :] = value

    inner = half - out_cells
    for k in range(chunks // 2 + 1):
        mask_chunk(k)
    pl.semaphore_wait(barrier, len(peers))
    came = [
        push(snapshots.at[pl.ds(rows_dev - 2, 2)], field.at[pl.ds(0, 2)], below, field.at[pl.ds(0, 2)]),
        push(snapshots.at[pl.ds(0, 2)], field.at[pl.ds(rows_dev + 2, 2)], above, field.at[pl.ds(rows_dev + 2, 2)]),
        push(mask.at[pl.ds(rows_dev - 8, 8)], mask_ends.at[pl.ds(0, 8)], below, mask_ends.at[pl.ds(0, 8)]),
        push(mask.at[pl.ds(0, 8)], mask_ends.at[pl.ds(8, 8)], above, mask_ends.at[pl.ds(8, 8)]),
    ]
    filter_rows(1 + (out_rows // 2 - 1) * (1 - core), store_away)
    crossed = [
        push(
            away.at[rows_at(core * out_cells, inner)],
            pair.at[core, rows_at(core * out_cells, inner)],
            at(flip=1),
            pair.at[1 - core, rows_at((1 - core) * out_cells, inner)],
        )
    ]
    for k in range(chunks // 2 + 1, chunks):
        mask_chunk(k)
    filter_rows(1 + (out_rows // 2 - 1) * core, store_own)
    arrive(came)
    ends = mask_ends[...].astype(jnp.float32)
    ends = jnp.concatenate(
        [jnp.where(s > 0, ends[:8], 0.0), jnp.where(s < SPACE - 1, ends[8:], 0.0), jnp.zeros((COLS - 16, cells), jnp.float32)],
        axis=0,
    ).T
    for row, lane in ((0, 6), (1, 7), (rows_dev + 2, 8), (rows_dev + 3, 9)):
        field[row] = field[row] * ends[:, lane : lane + 1]
    last_away = rows_at((out_rows // 2 - 1) * out_cells * (1 - core), out_cells)
    last_own = rows_at((out_rows // 2 - 1) * out_cells * core, out_cells)
    away[last_away, :] = filter_row((out_rows - 1) * (1 - core), 0)
    crossed.append(
        push(away.at[last_away], pair.at[core, last_away], at(flip=1), pair.at[1 - core, last_own])
    )
    pair[core, last_own, :] = filter_row((out_rows - 1) * core, 1)
    arrive(crossed)

    def plane_sum(part, gath, cbuf, zbuf, xbuf):
        rows = part.shape[0] // 2
        piece = rows // NZ_CHIPS
        mine = core * rows
        arrive([push(part.at[rows_at((1 - core) * rows, rows)], cbuf, at(flip=1), cbuf)])
        part[rows_at(mine, rows), :] = part[rows_at(mine, rows), :] + cbuf[...]
        arrive([
            push(part.at[rows_at(mine + (z + d) % NZ_CHIPS * piece, piece)], zbuf.at[d - 1], at(d_z=d), zbuf.at[d - 1])
            for d in z_offsets
        ])
        total = part[rows_at(mine + z * piece, piece), :]
        for d in z_offsets:
            total = total + zbuf[d - 1]
        xbuf[x] = total
        arrive([
            push(xbuf.at[x], xbuf.at[x], at(d_x=d), xbuf.at[(x + NX_CHIPS - d) % NX_CHIPS]) for d in x_offsets
        ])
        total = (xbuf[0] + xbuf[1]) + (xbuf[2] + xbuf[3])
        own = gath.at[rows_at(mine + z * piece, piece)]
        gath[rows_at(mine + z * piece, piece), :] = total
        arrive([
            push(own, own, at(d_z=d), gath.at[rows_at(mine + (z + NZ_CHIPS - d) % NZ_CHIPS * piece, piece)])
            for d in z_offsets
        ])
        ours, theirs = gath.at[rows_at(mine, rows)], gath.at[rows_at((1 - core) * rows, rows)]
        arrive([push(ours, ours, at(flip=1), theirs)])

    class WholeSum:
        def __init__(self, part, gath, cbuf, rbuf, zbuf):
            self.part, self.gath, self.cbuf, self.rbuf, self.zbuf = part, gath, cbuf, rbuf, zbuf
            self.rows = part.shape[0] // 2
            self.piece = self.rows // XY_CHIPS
            self.ours = rows_at(core * self.rows, self.rows)
            self.theirs = rows_at((1 - core) * self.rows, self.rows)

        def piece_of(self, a, b):
            owner = (x + a) % NX_CHIPS * NY_CHIPS + (y + b) % NY_CHIPS
            return rows_at(core * self.rows + owner * self.piece, self.piece)

        def start(self):
            self.came = [push(self.part.at[self.theirs], self.cbuf, at(flip=1), self.cbuf)]

        def scatter(self):
            arrive(self.came)
            self.part[self.ours, :] = self.part[self.ours, :] + self.cbuf[...]
            self.came = [
                push(self.part.at[self.piece_of(a, b)], self.rbuf.at[n], at(d_x=a, d_y=b), self.rbuf.at[n])
                for n, (a, b) in enumerate(xy_offsets)
            ]

        def along_z(self):
            arrive(self.came)
            total = self.part[self.piece_of(0, 0), :]
            for n in range(len(xy_offsets)):
                total = total + self.rbuf[n]
            self.zbuf[z] = total
            self.came = [
                push(self.zbuf.at[z], self.zbuf.at[z], at(d_z=d), self.zbuf.at[(z + NZ_CHIPS - d) % NZ_CHIPS])
                for d in z_offsets
            ]

        def gather(self):
            arrive(self.came)
            terms = [self.zbuf[k] for k in range(NZ_CHIPS)]
            while len(terms) > 1:
                terms = [terms[k] + terms[k + 1] for k in range(0, len(terms), 2)]
            own = self.piece_of(0, 0)
            self.gath[own, :] = terms[0]
            own = self.gath.at[own]
            self.came = [
                push(own, own, at(d_x=a, d_y=b), self.gath.at[self.piece_of(NX_CHIPS - a, NY_CHIPS - b)])
                for a, b in xy_offsets
            ]

        def share(self):
            arrive(self.came)
            ours, theirs = self.gath.at[self.ours], self.gath.at[self.theirs]
            self.came = [push(ours, ours, at(flip=1), theirs)]

        def finish(self):
            arrive(self.came)

    gram[...] = jnp.zeros_like(gram)

    def add_rows(chunk, carry):
        rows = rows_at(chunk * own_rows, own_rows)
        high, low = halves(jnp.concatenate([pair[0, rows, :], pair[1, rows, :]], axis=1))
        cat_high[rows, :] = high
        cat_low[rows, :] = low
        cross = dot(high, low, TN)
        gram[...] = gram[...] + (dot(high, high, TN) + (cross + cross.T))
        return carry

    lax.fori_loop(0, NY_CHIPS, add_rows, 0)
    part1[:COLS] = gram[:COLS, :COLS]
    part1[COLS : 2 * COLS] = gram[:COLS, COLS:]
    part1[2 * COLS :] = gram[COLS:, COLS:]
    plane_sum(part1, gath1, cbuf1, zbuf1, xbuf1)
    total = block_2x2(gath1[:COLS], gath1[COLS : 2 * COLS], gath1[2 * COLS :])
    start_sign(total, sign.at[0])
    run_signs(SIGN_STEPS, sign.at[0])
    combine = combine_of(sign.at[0])
    combine_halves = halves(combine)

    came = []
    for d in [1, 2, 3, 0]:
        to = (y + d) % NY_CHIPS
        rows = rows_at(to * own_rows, own_rows)
        merged = dot3((cat_high[rows, :], cat_low[rows, :]), combine_halves)
        if d:
            quarter[d - 1] = merged
            came.append(push(quarter.at[d - 1], rows4.at[y], at(d_y=d), rows4.at[(y + NY_CHIPS - d) % NY_CHIPS]))
        else:
            rows4[y] = merged
    diag[y] = mul(combine, mul(total, combine), TN)
    diag_came = [
        push(diag.at[y], diag.at[y], at(d_y=d), diag.at[(y + NY_CHIPS - d) % NY_CHIPS]) for d in y_offsets
    ]
    take_probes.wait()
    arrive(came)

    f4 = [halves(rows4[p]) for p in range(NY_CHIPS)]
    probe_halves = halves(probe_rows[...])
    sum_now = WholeSum(part2, gath2, cbuf2, rbuf2, zbuf2)
    sum_later = WholeSum(part3, gath3, cbuf3, rbuf3, zbuf3)
    part2[:COLS] = dot3(f4[0], f4[1], TN)
    part2[COLS:] = dot3(f4[2], f4[3], TN)
    sum_now.start()
    place = {(0, 2): 0, (0, 3): 1, (1, 2): 2, (1, 3): 3, (0, 4): 4, (1, 4): 5, (2, 4): 6, (3, 4): 7}
    right = f4 + [probe_halves]

    def later_blocks(p):
        first = 2 if p < 2 else 4
        wide = tuple(jnp.concatenate([right[q][h] for q in range(first, 5)], axis=1) for h in range(2))
        products = dot3(f4[p], wide, TN)
        for q in range(first, 5):
            at_block = place[p, q] * COLS
            part3[at_block : at_block + COLS] = products[:, (q - first) * COLS : (q - first + 1) * COLS]

    sum_now.scatter()
    for p in range(NY_CHIPS):
        later_blocks(p)
    sum_later.start()
    sum_later.scatter()
    sum_now.along_z()
    sum_later.along_z()
    sum_now.gather()
    sum_later.gather()
    sum_now.share()
    arrive(diag_came)
    sum_now.finish()

    def summed(index):
        return gath3[index * COLS : (index + 1) * COLS]

    gram_low = block_2x2(diag[0], gath2[:COLS], diag[1])
    gram_high = block_2x2(diag[2], gath2[COLS:], diag[3])
    start_sign(gram_low, sign.at[0])
    start_sign(gram_high, sign.at[1])
    run_signs(6, sign.at[0], sign.at[1])
    sum_later.share()
    run_signs(SIGN_STEPS - 6, sign.at[0], sign.at[1])
    sum_later.finish()
    low, high = combine_of(sign.at[0]), combine_of(sign.at[1])
    low_h, high_h = halves(low), halves(high)
    crossing = jnp.concatenate(
        [jnp.concatenate([summed(0), summed(1)], axis=1), jnp.concatenate([summed(2), summed(3)], axis=1)], axis=0
    )
    diag_low = dot3(low_h, halves(dot3(halves(gram_low), low_h)), TN)
    diag_high = dot3(high_h, halves(dot3(halves(gram_high), high_h)), TN)
    cross = dot3(low_h, halves(dot3(halves(crossing), high_h)), TN)

    start_sign(block_2x2(diag_low, cross, diag_high), sign.at[0])
    run_signs(SIGN_STEPS, sign.at[0])
    last = combine_of(sign.at[0])
    whole = halves(
        jnp.concatenate([dot3(low_h, halves(last[:COLS])), dot3(high_h, halves(last[COLS:]))], axis=0)
    )
    all4 = tuple(jnp.concatenate([f[h] for f in [halves(rows4[p]) for p in range(NY_CHIPS)]], axis=1) for h in range(2))
    basis = dot3(all4, whole)
    for k in range(own_rows // out_cells):
        turned[k] = basis[k * out_cells : (k + 1) * out_cells].T
    width = COLS // 8

    def grid_rows(place):
        count = own_rows // out_cells
        return pl.ds(place * count, count)

    place_own = core * NY_CHIPS + y
    came = []
    for f in range(2):
        for d in range(NY_CHIPS):
            if d or f:
                to_t = ((y + d) % NY_CHIPS) * 2 + (core + f) % 2
                from_place = ((core + f) % 2) * NY_CHIPS + (y + NY_CHIPS - d) % NY_CHIPS
                came.append(
                    push(
                        turned.at[:, rows_at(to_t * width, width)], pieces.at[grid_rows(place_own)], at(d_y=d, flip=f),
                        pieces.at[grid_rows(from_place)],
                    )
                )
    pieces[grid_rows(place_own)] = turned[:, rows_at(t * width, width), :]
    coef_all[...] = dot3(whole, halves(gath3[4 * COLS :]), TN)
    coef[...] = coef_all[rows_at(t * width, width), :]
    arrive(came)
    for out in unsent:
        out.wait_send()


def merge_all(snapshots, mask, taps_rows, taps_cols, probes):
    rows_dev, cells, cols = snapshots.shape
    rows = rows_dev // 2 * (cells // 2)
    half = rows // 2
    own_rows = half // NY_CHIPS
    f32, vmem = jnp.float32, pltpu.VMEM
    piece1 = FIRST_ROWS // 2 // NZ_CHIPS
    piece2, piece3 = SECOND_ROWS // 2 // XY_CHIPS, LATER_ROWS // 2 // XY_CHIPS
    return pl.pallas_call(
        merge_kernel,
        out_shape=(
            jax.ShapeDtypeStruct((rows_dev // 2, cols // 8, cells // 2), f32),
            jax.ShapeDtypeStruct((cols // 8, cols), f32),
        ),
        in_specs=[pl.BlockSpec(memory_space=pl.ANY)] * 5,
        out_specs=(pl.BlockSpec(memory_space=pltpu.VMEM), pl.BlockSpec(memory_space=pltpu.VMEM)),
        scratch_shapes=[
            pltpu.SMEM((TAPS,), f32),
            pltpu.SMEM((TAPS,), f32),
            vmem((rows_dev + 4, cells, cols), f32),
            vmem((COLS, cells), jnp.int32),
            vmem((16, cells), jnp.int32),
            vmem((3, cells + 2 * EDGE, cols), f32),
            vmem((half, cols), f32),
            vmem((2, half, cols), f32),
            vmem((half, 2 * cols), jnp.bfloat16),
            vmem((half, 2 * cols), jnp.bfloat16),
            vmem((2 * cols, 2 * cols), f32),
            vmem((FIRST_ROWS, cols), f32),
            vmem((FIRST_ROWS, cols), f32),
            vmem((FIRST_ROWS // 2, cols), f32),
            vmem((NZ_CHIPS - 1, piece1, cols), f32),
            vmem((NX_CHIPS, piece1, cols), f32),
            vmem((NY_CHIPS - 1, own_rows, cols), f32),
            vmem((NY_CHIPS, own_rows, cols), f32),
            vmem((NY_CHIPS, cols, cols), f32),
            vmem((SECOND_ROWS, cols), f32),
            vmem((SECOND_ROWS, cols), f32),
            vmem((SECOND_ROWS // 2, cols), f32),
            vmem((XY_CHIPS - 1, piece2, cols), f32),
            vmem((NZ_CHIPS, piece2, cols), f32),
            vmem((LATER_ROWS, cols), f32),
            vmem((LATER_ROWS, cols), f32),
            vmem((LATER_ROWS // 2, cols), f32),
            vmem((XY_CHIPS - 1, piece3, cols), f32),
            vmem((NZ_CHIPS, piece3, cols), f32),
            vmem((2, 2 * cols, 2 * cols), f32),
            vmem((own_rows, cols), f32),
            vmem((own_rows * 2 // cells, cols, cells // 2), f32),
            vmem((cols, cols), f32),
            pltpu.SemaphoreType.DMA((128,)),
            pltpu.SemaphoreType.DMA((128,)),
            pltpu.SemaphoreType.DMA((4,)),
            pltpu.SemaphoreType.DMA((rows_dev // CHUNK,)),
        ],
        compiler_params=pltpu.CompilerParams(
            collective_id=1, has_side_effects=True
        ),
        name="merge_all",
    )(snapshots, mask, taps_rows, taps_cols, probes)


def local(snapshots, land_mask, taps_rows, taps_cols, probes):
    rows_dev, cell_cols, columns = snapshots.shape
    cell_rows = rows_dev // 2 * (cell_cols // 2)
    flat_probes = probes.reshape(cell_rows, probes.shape[2])
    pieces, coef_own = merge_all(snapshots, land_mask, taps_rows, taps_cols, flat_probes)
    return (pieces.transpose(0, 2, 1), coef_own)


def solution(mesh):
    placed = (P("space", None, "tm"), P("space", None), P(), P(), P("space", None, None))
    return jax.shard_map(
        local,
        mesh=mesh,
        in_specs=placed,
        out_specs=(P("space", None, "tm"), P("tm", None)),
        check_vma=False,
    )
```

```python
import functools

import jax
import jax.numpy as jnp
from jax import lax
from jax.experimental import pallas as pl
from jax.experimental.pallas import tpu as pltpu
from jax.sharding import PartitionSpec as P

SIGN_STEPS = 8
GROUPS = 21
NX_CHIPS, NY_CHIPS, NZ_CHIPS = 4, 4, 8
SPACE, XY_CHIPS = NX_CHIPS * NZ_CHIPS, NX_CHIPS * NY_CHIPS
COLS = 128
FIRST_ROWS, SECOND_ROWS, LATER_ROWS = 3 * COLS, 2 * COLS, 8 * COLS
TAPS, CHUNK, EDGE, MARGIN = 6, 8, 8, 4
MESH = pl.DeviceIdType.MESH

def rows_at(start, size):
    return pl.ds(pl.multiple_of(start, 8), size)


NN = (((1,), (0,)), ((), ()))
TN = (((0,), (0,)), ((), ()))


def halves(a):
    high = a.astype(jnp.bfloat16)
    return high, (a - high.astype(jnp.float32)).astype(jnp.bfloat16)


def dot(a, b, dims):
    return lax.dot_general(a, b, dims, preferred_element_type=jnp.float32)


def dot3(a, b, dims=NN):
    (a_high, a_low), (b_high, b_low) = a, b
    (a_dim,), (b_dim,) = dims[0]
    left = jnp.concatenate([a_high, a_low, a_high], axis=a_dim)
    right = jnp.concatenate([b_high, b_high, b_low], axis=b_dim)
    return dot(left, right, dims)


def mul(a, b, dims=NN):
    return dot3(halves(a), halves(b), dims)


def block_2x2(low, cross, high):
    return jnp.concatenate(
        [jnp.concatenate([low, cross], axis=1), jnp.concatenate([cross.T, high], axis=1)], axis=0
    )


def start_sign(gram, y_ref):
    order = gram.shape[0]
    identity = lax.broadcasted_iota(jnp.int32, gram.shape, 0) == lax.broadcasted_iota(jnp.int32, gram.shape, 1)
    mean_eig = jnp.sum(jnp.where(identity, gram, 0.0), keepdims=True) / order
    shifted = gram - jnp.where(identity, mean_eig, 0.0)
    y_ref[...] = shifted / jnp.sqrt(jnp.sum(shifted * shifted, keepdims=True) + 1e-06)


def sign_step(y_ref):
    y = y_ref[...]
    y_halves = halves(y)
    square = dot3(y_halves, y_halves)
    y_ref[...] = 1.5 * y - 0.5 * dot3(y_halves, halves(square))


def combine_of(y_ref):
    y = y_ref[...]
    order = y.shape[0]
    row = lax.broadcasted_iota(jnp.int32, (order, order // 2), 0)
    col = lax.broadcasted_iota(jnp.int32, (order, order // 2), 1)
    ones = jnp.where((row == col) | (row == col + order // 2), 0.5, 0.0)
    return ones + 0.5 * (y[:, : order // 2] + y[:, order // 2 :])


def run_signs(steps, *refs):
    def body(step, carry):
        for ref in refs:
            sign_step(ref)
        return carry

    lax.fori_loop(0, steps, body, 0)


def merge_kernel(snapshots, mask, taps_rows, taps_cols, probes, pieces, coef,
                 row_taps, col_taps, field, mask_own, tall, edges, edge_in, away, pair, cat_high, cat_low, gram, part1, gath1, cbuf1, zbuf1, xbuf1,
                 quarter, rows4, diag, part2, gath2, cbuf2, rbuf2, zbuf2,
                 part3, gath3, cbuf3, rbuf3, zbuf3, sign, probe_rows, turned, coef_all, combines, diag_next,
                 send, recv, local_sem, chunk_sem):
    t = lax.axis_index("tm")
    s = lax.axis_index("space")
    y, core = t // 2, t % 2
    x, z = s // NZ_CHIPS, s % NZ_CHIPS
    rows_dev, cells = snapshots.shape[0], snapshots.shape[1]
    out_rows, out_cells = rows_dev // 2, cells // 2
    half = out_rows * out_cells // 2
    chunks = rows_dev // CHUNK
    own_rows = half // NY_CHIPS

    def at(d_z=0, d_x=0, d_y=0, flip=0):
        c = (core + flip) % 2
        return {
            "tm": ((y + d_y) % NY_CHIPS) * 2 + c,
            "space": ((x + d_x) % NX_CHIPS) * NZ_CHIPS + (z + d_z) % NZ_CHIPS,
        }

    z_offsets = range(1, NZ_CHIPS)
    x_offsets = range(1, NX_CHIPS)
    y_offsets = range(1, NY_CHIPS)
    s_above, s_below = (s + SPACE - 1) % SPACE, (s + 1) % SPACE
    barrier = pltpu.get_barrier_semaphore()
    xy_offsets = [(a, b) for a in range(NX_CHIPS) for b in range(NY_CHIPS) if a or b]
    peers = [at(d_z=d) for d in z_offsets] + [at(d_x=a, d_y=b) for a, b in xy_offsets]
    peers += [at(d_y=d, flip=1) for d in range(NY_CHIPS)]
    peers += [{"tm": 2 * y + c, "space": there} for c in range(2) for there in (s_above, s_below)]
    for peer in peers:
        pl.semaphore_signal(barrier, inc=1, device_id=peer, device_id_type=MESH)

    count = [0]
    unsent = []

    class Group:
        def __init__(self, landed):
            self.index, self.landed = count[0], landed
            count[0] += 1
            unsent.append(self)

        def make(self, src, dst, to):
            return pltpu.make_async_remote_copy(
                src_ref=src, dst_ref=dst, send_sem=send.at[self.index], recv_sem=recv.at[self.index],
                device_id=to, device_id_type=MESH,
            )

        def push(self, src, dst, to):
            self.make(src, dst, to).start()
            return self

        def arrive(self):
            self.make(self.landed, self.landed, at(flip=1)).wait_recv()

        def wait_send(self):
            self.make(self.landed, self.landed, at(flip=1)).wait_send()

    def push(src, dst, to, landed):
        return Group(landed).push(src, dst, to)

    take_probes = pltpu.make_async_copy(
        probes.at[rows_at(core * half + y * own_rows, own_rows)], probe_rows, local_sem.at[0]
    )
    take_probes.start()
    take_mask = pltpu.make_async_copy(mask, mask_own.at[pl.ds(0, rows_dev)], local_sem.at[1])
    take_mask.start()
    take_taps = [
        pltpu.make_async_copy(taps_rows, row_taps, local_sem.at[2]),
        pltpu.make_async_copy(taps_cols, col_taps, local_sem.at[3]),
    ]
    for taps in take_taps:
        taps.start()

    order = [0, chunks - 1] + list(range(1, chunks - 1))

    def chunk_first(k):
        return (core * k + (1 - core) * (chunks - 1 - k)) * CHUNK

    def chunk_copy(k):
        first = chunk_first(k)
        return pltpu.make_async_copy(
            snapshots.at[pl.ds(first, CHUNK)], field.at[pl.ds(first + MARGIN, CHUNK)], chunk_sem.at[k]
        )

    for k in order:
        chunk_copy(k).start()
    for margin in (0, MARGIN + rows_dev):
        field[pl.ds(margin, MARGIN)] = jnp.zeros((MARGIN, cells, COLS), jnp.float32)
    mask_own[rows_dev:, :] = jnp.zeros((COLS - rows_dev, cells), jnp.int32)
    tall[:, :EDGE] = jnp.zeros((tall.shape[0], EDGE, COLS), jnp.float32)
    tall[:, EDGE + cells :] = jnp.zeros((tall.shape[0], EDGE, COLS), jnp.float32)
    take_mask.wait()
    mask_cols = mask_own[...].astype(jnp.float32).T

    def mask_chunk(k):
        chunk_copy(k).wait()
        first = chunk_first(k)
        turned_mask = pltpu.roll(mask_cols, (COLS - first) % COLS, axis=1)
        for r in range(CHUNK):
            field[first + MARGIN + r] = field[first + MARGIN + r] * turned_mask[:, r : r + 1]

    for taps in take_taps:
        taps.wait()
    tr = [row_taps[k] for k in range(TAPS)]
    tc = [col_taps[k] for k in range(TAPS)]

    def filter_row(i, slot):
        total = tr[0] * field[2 * i + MARGIN - 2]
        for k in range(1, TAPS):
            total = total + tr[k] * field[2 * i + MARGIN - 2 + k]
        tall[slot, EDGE : EDGE + cells] = total
        out = tc[0] * tall[slot, pl.ds(EDGE - 2, out_cells, stride=2), :]
        for k in range(1, TAPS):
            out = out + tc[k] * tall[slot, pl.ds(EDGE - 2 + k, out_cells, stride=2), :]
        return out

    def filter_half(which, store):
        slots = tall.shape[0]

        def body(step, carry):
            for slot in range(slots):
                n = step * slots + slot
                store(rows_at(n * out_cells, out_cells), filter_row(which * (out_rows // 2) + n, slot))
            return carry

        lax.fori_loop(0, out_rows // 2 // slots, body, 0)

    def store_away(rows, value):
        away[rows, :] = value

    def store_own(rows, value):
        pair[core, rows, :] = value

    for k in order[:2]:
        mask_chunk(k)
    edges[0] = filter_row(-1, 0)
    edges[1] = filter_row(out_rows, 1)
    for k in order[2 : chunks // 2 + 2]:
        mask_chunk(k)
    filter_half(1 - core, store_away)
    pl.semaphore_wait(barrier, len(peers))
    crossed = push(away, pair.at[core], at(flip=1), pair.at[1 - core])
    edge_group = Group(edge_in)
    edge_group.push(edges.at[0], edge_in.at[core], {"tm": 2 * y + 1, "space": s_above})
    edge_group.push(edges.at[1], edge_in.at[core], {"tm": 2 * y, "space": s_below})
    for k in order[chunks // 2 + 2 :]:
        mask_chunk(k)
    filter_half(core, store_own)
    edge_group.arrive()
    crossed.arrive()
    touches = ((s > 0) & (core == 0)) | ((s < SPACE - 1) & (core == 1))
    edge_rows = rows_at((out_rows // 2 - 1) * out_cells * core, out_cells)
    for c in range(2):
        pair[c, edge_rows, :] = pair[c, edge_rows, :] + jnp.where(touches, edge_in[c], 0.0)

    def plane_sum(part, gath, cbuf, zbuf, xbuf):
        rows = part.shape[0] // 2
        piece = rows // NZ_CHIPS
        mine = core * rows
        push(part.at[rows_at((1 - core) * rows, rows)], cbuf, at(flip=1), cbuf).arrive()
        part[rows_at(mine, rows), :] = part[rows_at(mine, rows), :] + cbuf[...]
        group = Group(zbuf)
        for d in z_offsets:
            group.push(part.at[rows_at(mine + (z + d) % NZ_CHIPS * piece, piece)], zbuf.at[d - 1], at(d_z=d))
        group.arrive()
        total = part[rows_at(mine + z * piece, piece), :]
        for d in z_offsets:
            total = total + zbuf[d - 1]
        xbuf[x] = total
        group = Group(xbuf.at[pl.ds(0, NX_CHIPS - 1)])
        for d in x_offsets:
            group.push(xbuf.at[x], xbuf.at[x], at(d_x=d))
        group.arrive()
        own = gath.at[rows_at(mine + z * piece, piece)]
        gath[rows_at(mine + z * piece, piece), :] = (xbuf[0] + xbuf[1]) + (xbuf[2] + xbuf[3])
        group = Group(gath.at[rows_at(mine, (NZ_CHIPS - 1) * piece)])
        for d in z_offsets:
            group.push(own, own, at(d_z=d))
        group.arrive()
        ours, theirs = gath.at[rows_at(mine, rows)], gath.at[rows_at((1 - core) * rows, rows)]
        push(ours, ours, at(flip=1), theirs).arrive()

    class WholeSum:
        def __init__(self, part, gath, cbuf, rbuf, zbuf):
            self.part, self.gath, self.cbuf, self.rbuf, self.zbuf = part, gath, cbuf, rbuf, zbuf
            self.rows = part.shape[0] // 2
            self.piece = self.rows // XY_CHIPS
            self.ours = rows_at(core * self.rows, self.rows)
            self.theirs = rows_at((1 - core) * self.rows, self.rows)

        def piece_of(self, a, b):
            owner = (x + a) % NX_CHIPS * NY_CHIPS + (y + b) % NY_CHIPS
            return rows_at(core * self.rows + owner * self.piece, self.piece)

        def start(self):
            self.came = push(self.part.at[self.theirs], self.cbuf, at(flip=1), self.cbuf)

        def scatter(self):
            self.came.arrive()
            self.part[self.ours, :] = self.part[self.ours, :] + self.cbuf[...]
            self.came = Group(self.rbuf)
            for n, (a, b) in enumerate(xy_offsets):
                self.came.push(self.part.at[self.piece_of(a, b)], self.rbuf.at[n], at(d_x=a, d_y=b))

        def along_z(self):
            self.came.arrive()
            total = self.part[self.piece_of(0, 0), :]
            for n in range(len(xy_offsets)):
                total = total + self.rbuf[n]
            self.zbuf[z] = total
            self.came = Group(self.zbuf.at[pl.ds(0, NZ_CHIPS - 1)])
            for d in z_offsets:
                self.came.push(self.zbuf.at[z], self.zbuf.at[z], at(d_z=d))

        def gather(self):
            self.came.arrive()
            terms = [self.zbuf[k] for k in range(NZ_CHIPS)]
            while len(terms) > 1:
                terms = [terms[k] + terms[k + 1] for k in range(0, len(terms), 2)]
            own = self.piece_of(0, 0)
            self.gath[own, :] = terms[0]
            own = self.gath.at[own]
            self.came = Group(self.gath.at[rows_at(core * self.rows, (XY_CHIPS - 1) * self.piece)])
            for a, b in xy_offsets:
                self.came.push(own, own, at(d_x=a, d_y=b))

        def share(self):
            self.came.arrive()
            ours, theirs = self.gath.at[self.ours], self.gath.at[self.theirs]
            self.came = push(ours, ours, at(flip=1), theirs)

        def finish(self):
            self.came.arrive()

    gram[...] = jnp.zeros_like(gram)

    def add_rows(chunk, carry):
        rows = rows_at(chunk * own_rows, own_rows)
        high, low = halves(jnp.concatenate([pair[0, rows, :], pair[1, rows, :]], axis=1))
        cat_high[rows, :] = high
        cat_low[rows, :] = low
        cross = dot(high, low, TN)
        gram[...] = gram[...] + (dot(high, high, TN) + (cross + cross.T))
        return carry

    lax.fori_loop(0, NY_CHIPS, add_rows, 0)
    part1[:COLS] = gram[:COLS, :COLS]
    part1[COLS : 2 * COLS] = gram[:COLS, COLS:]
    part1[2 * COLS :] = gram[COLS:, COLS:]
    plane_sum(part1, gath1, cbuf1, zbuf1, xbuf1)
    total = block_2x2(gath1[:COLS], gath1[COLS : 2 * COLS], gath1[2 * COLS :])
    start_sign(total, sign.at[0])
    run_signs(SIGN_STEPS, sign.at[0])
    combine = combine_of(sign.at[0])
    combine_halves = halves(combine)

    quarters = Group(rows4.at[pl.ds(0, NY_CHIPS - 1)])
    for d in [2, 1, 3, 0]:
        to = (y + d) % NY_CHIPS
        rows = rows_at(to * own_rows, own_rows)
        merged = dot3((cat_high[rows, :], cat_low[rows, :]), combine_halves)
        if d:
            quarter[d - 1] = merged
            quarters.push(quarter.at[d - 1], rows4.at[y], at(d_y=d))
        else:
            rows4[y] = merged
    diag[y] = mul(combine, mul(total, combine), TN)
    diags = Group(diag.at[pl.ds(0, NY_CHIPS - 1)])
    for d in y_offsets:
        diags.push(diag.at[y], diag.at[y], at(d_y=d))
    take_probes.wait()
    quarters.arrive()

    f4 = [halves(rows4[p]) for p in range(NY_CHIPS)]
    probe_halves = halves(probe_rows[...])
    sum_now = WholeSum(part2, gath2, cbuf2, rbuf2, zbuf2)
    sum_later = WholeSum(part3, gath3, cbuf3, rbuf3, zbuf3)

    def beside(*blocks):
        return tuple(jnp.concatenate([block[h] for block in blocks], axis=1) for h in range(2))

    products = dot3(beside(f4[0], f4[2]), beside(f4[1], f4[3]), TN)
    part2[:COLS] = products[:COLS, :COLS]
    part2[COLS:] = products[COLS:, COLS:]
    sum_now.start()
    sum_now.scatter()
    products = dot3(beside(f4[0], f4[1]), beside(f4[2], f4[3], probe_halves), TN)
    for n, (p, q) in enumerate([(0, 0), (0, 1), (1, 0), (1, 1), (0, 2), (1, 2)]):
        part3[n * COLS : (n + 1) * COLS] = products[p * COLS : (p + 1) * COLS, q * COLS : (q + 1) * COLS]
    part3[6 * COLS :] = dot3(beside(f4[2], f4[3]), probe_halves, TN)
    sum_later.start()
    sum_later.scatter()
    sum_now.along_z()
    sum_later.along_z()
    sum_now.gather()
    sum_later.gather()
    sum_now.share()
    diags.arrive()
    sum_now.finish()

    def summed(index):
        return gath3[index * COLS : (index + 1) * COLS]

    def gram_of(which):
        return block_2x2(diag[2 * which], gath2[rows_at(which * COLS, COLS), :], diag[2 * which + 1])

    def diag_of(which):
        c = halves(combines[which])
        return dot3(c, halves(dot3(halves(gram_of(which)), c)), TN)

    start_sign(gram_of(core), sign.at[0])
    run_signs(6, sign.at[0])
    sum_later.share()
    run_signs(SIGN_STEPS - 6, sign.at[0])
    combines[core] = combine_of(sign.at[0])
    swapped = push(combines.at[core], combines.at[core], at(flip=1), combines.at[1 - core])
    diag_next[core] = diag_of(core)
    sum_later.finish()
    swapped.arrive()
    diag_next[1 - core] = diag_of(1 - core)
    low_h, high_h = halves(combines[0]), halves(combines[1])
    crossing = jnp.concatenate(
        [jnp.concatenate([summed(0), summed(1)], axis=1), jnp.concatenate([summed(2), summed(3)], axis=1)], axis=0
    )
    cross = dot3(low_h, halves(dot3(halves(crossing), high_h)), TN)

    start_sign(block_2x2(diag_next[0], cross, diag_next[1]), sign.at[0])
    run_signs(SIGN_STEPS, sign.at[0])
    last = combine_of(sign.at[0])
    whole = halves(
        jnp.concatenate([dot3(low_h, halves(last[:COLS])), dot3(high_h, halves(last[COLS:]))], axis=0)
    )
    all4 = tuple(jnp.concatenate([f[h] for f in [halves(rows4[p]) for p in range(NY_CHIPS)]], axis=1) for h in range(2))
    basis = dot3(all4, whole)
    for k in range(own_rows // out_cells):
        turned[k] = basis[k * out_cells : (k + 1) * out_cells].T
    width = COLS // 8

    def grid_rows(place):
        count = own_rows // out_cells
        return pl.ds(place * count, count)

    place_own = core * NY_CHIPS + y
    outward = Group(pieces.at[pl.ds(0, out_rows - out_rows // 8)])
    for f in range(2):
        for d in range(NY_CHIPS):
            if d or f:
                to_t = ((y + d) % NY_CHIPS) * 2 + (core + f) % 2
                outward.push(
                    turned.at[:, rows_at(to_t * width, width)], pieces.at[grid_rows(place_own)], at(d_y=d, flip=f)
                )
    pieces[grid_rows(place_own)] = turned[:, rows_at(t * width, width), :]
    coef_all[...] = dot3(whole, halves(gath3[4 * COLS :]), TN)
    coef[...] = coef_all[rows_at(t * width, width), :]
    outward.arrive()
    assert count[0] == GROUPS
    for out in unsent:
        out.wait_send()


def merge_all(snapshots, mask, taps_rows, taps_cols, probes):
    rows_dev, cells, cols = snapshots.shape
    rows = rows_dev // 2 * (cells // 2)
    half = rows // 2
    own_rows = half // NY_CHIPS
    f32, vmem = jnp.float32, pltpu.VMEM
    piece1 = FIRST_ROWS // 2 // NZ_CHIPS
    piece2, piece3 = SECOND_ROWS // 2 // XY_CHIPS, LATER_ROWS // 2 // XY_CHIPS
    return pl.pallas_call(
        merge_kernel,
        out_shape=(
            pltpu.VMEM((rows_dev // 2, cols // 8, cells // 2), f32),
            pltpu.VMEM((cols // 8, cols), f32),
        ),
        in_specs=[pl.BlockSpec(memory_space=pl.ANY)] * 5,
        out_specs=(pl.BlockSpec(memory_space=pltpu.VMEM), pl.BlockSpec(memory_space=pltpu.VMEM)),
        scratch_shapes=[
            pltpu.SMEM((TAPS,), f32),
            pltpu.SMEM((TAPS,), f32),
            vmem((rows_dev + 2 * MARGIN, cells, cols), f32),
            vmem((COLS, cells), jnp.int32),
            vmem((4, cells + 2 * EDGE, cols), f32),
            vmem((2, cells // 2, cols), f32),
            vmem((2, cells // 2, cols), f32),
            vmem((half, cols), f32),
            vmem((2, half, cols), f32),
            vmem((half, 2 * cols), jnp.bfloat16),
            vmem((half, 2 * cols), jnp.bfloat16),
            vmem((2 * cols, 2 * cols), f32),
            vmem((FIRST_ROWS, cols), f32),
            vmem((FIRST_ROWS, cols), f32),
            vmem((FIRST_ROWS // 2, cols), f32),
            vmem((NZ_CHIPS - 1, piece1, cols), f32),
            vmem((NX_CHIPS, piece1, cols), f32),
            vmem((NY_CHIPS - 1, own_rows, cols), f32),
            vmem((NY_CHIPS, own_rows, cols), f32),
            vmem((NY_CHIPS, cols, cols), f32),
            vmem((SECOND_ROWS, cols), f32),
            vmem((SECOND_ROWS, cols), f32),
            vmem((SECOND_ROWS // 2, cols), f32),
            vmem((XY_CHIPS - 1, piece2, cols), f32),
            vmem((NZ_CHIPS, piece2, cols), f32),
            vmem((LATER_ROWS, cols), f32),
            vmem((LATER_ROWS, cols), f32),
            vmem((LATER_ROWS // 2, cols), f32),
            vmem((XY_CHIPS - 1, piece3, cols), f32),
            vmem((NZ_CHIPS, piece3, cols), f32),
            vmem((1, 2 * cols, 2 * cols), f32),
            vmem((own_rows, cols), f32),
            vmem((own_rows * 2 // cells, cols, cells // 2), f32),
            vmem((cols, cols), f32),
            vmem((2, 2 * cols, cols), f32),
            vmem((2, cols, cols), f32),
            pltpu.SemaphoreType.DMA((GROUPS,)),
            pltpu.SemaphoreType.DMA((GROUPS,)),
            pltpu.SemaphoreType.DMA((4,)),
            pltpu.SemaphoreType.DMA((rows_dev // CHUNK,)),
        ],
        compiler_params=pltpu.CompilerParams(
            collective_id=1, has_side_effects=True
        ),
        name="merge_all",
    )(snapshots, mask, taps_rows, taps_cols, probes)


def local(snapshots, land_mask, taps_rows, taps_cols, probes):
    rows_dev, cell_cols, columns = snapshots.shape
    cell_rows = rows_dev // 2 * (cell_cols // 2)
    flat_probes = probes.reshape(cell_rows, probes.shape[2])
    pieces, coef_own = merge_all(snapshots, land_mask, taps_rows, taps_cols, flat_probes)
    return (pieces.transpose(0, 2, 1), coef_own)


def solution(mesh):
    placed = (P("space", None, "tm"), P("space", None), P(), P(), P("space", None, None))
    return jax.shard_map(
        local,
        mesh=mesh,
        in_specs=placed,
        out_specs=(P("space", None, "tm"), P("tm", None)),
        check_vma=False,
    )
```

```python
import functools

import jax
import jax.numpy as jnp
from jax import lax
from jax.experimental import pallas as pl
from jax.experimental.pallas import tpu as pltpu
from jax.sharding import PartitionSpec as P

SIGN_STEPS = 8
GROUPS = 21
NX_CHIPS, NY_CHIPS, NZ_CHIPS = 4, 4, 8
SPACE, XY_CHIPS = NX_CHIPS * NZ_CHIPS, NX_CHIPS * NY_CHIPS
COLS = 128
FIRST_ROWS, SECOND_ROWS, LATER_ROWS = 3 * COLS, 2 * COLS, 8 * COLS
TAPS, CHUNK, EDGE, MARGIN = 6, 8, 8, 4
MESH = pl.DeviceIdType.MESH

def rows_at(start, size):
    return pl.ds(pl.multiple_of(start, 8), size)


NN = (((1,), (0,)), ((), ()))
TN = (((0,), (0,)), ((), ()))


def halves(a):
    high = a.astype(jnp.bfloat16)
    return high, (a - high.astype(jnp.float32)).astype(jnp.bfloat16)


def dot(a, b, dims):
    return lax.dot_general(a, b, dims, preferred_element_type=jnp.float32)


def dot3(a, b, dims=NN):
    (a_high, a_low), (b_high, b_low) = a, b
    (a_dim,), (b_dim,) = dims[0]
    left = jnp.concatenate([a_high, a_low, a_high], axis=a_dim)
    right = jnp.concatenate([b_high, b_high, b_low], axis=b_dim)
    return dot(left, right, dims)


def mul(a, b, dims=NN):
    return dot3(halves(a), halves(b), dims)


def block_2x2(low, cross, high):
    return jnp.concatenate(
        [jnp.concatenate([low, cross], axis=1), jnp.concatenate([cross.T, high], axis=1)], axis=0
    )


def start_sign(gram, y_ref):
    order = gram.shape[0]
    identity = lax.broadcasted_iota(jnp.int32, gram.shape, 0) == lax.broadcasted_iota(jnp.int32, gram.shape, 1)
    mean_eig = jnp.sum(jnp.where(identity, gram, 0.0), keepdims=True) / order
    shifted = gram - jnp.where(identity, mean_eig, 0.0)
    y_ref[...] = shifted / jnp.sqrt(jnp.sum(shifted * shifted, keepdims=True) + 1e-06)


def sign_step(y_ref):
    y = y_ref[...]
    y_halves = halves(y)
    square = dot3(y_halves, y_halves)
    y_ref[...] = 1.5 * y - 0.5 * dot3(y_halves, halves(square))


def combine_of(y_ref):
    y = y_ref[...]
    order = y.shape[0]
    row = lax.broadcasted_iota(jnp.int32, (order, order // 2), 0)
    col = lax.broadcasted_iota(jnp.int32, (order, order // 2), 1)
    ones = jnp.where((row == col) | (row == col + order // 2), 0.5, 0.0)
    return ones + 0.5 * (y[:, : order // 2] + y[:, order // 2 :])


def run_signs(steps, *refs):
    def body(step, carry):
        for ref in refs:
            sign_step(ref)
        return carry

    lax.fori_loop(0, steps, body, 0)


def merge_kernel(snapshots, mask, taps_rows, taps_cols, probes, pieces, coef,
                 row_taps, col_taps, field, mask_own, tall, edges, edge_in, away, pair, cat_high, cat_low, gram, part1, gath1, cbuf1, zbuf1, xbuf1,
                 quarter, rows4, diag, part2, gath2, cbuf2, rbuf2, zbuf2,
                 part3, gath3, cbuf3, rbuf3, zbuf3, sign, probe_rows, turned, coef_all, combines, diag_next,
                 send, recv, local_sem, chunk_sem):
    t = lax.axis_index("tm")
    s = lax.axis_index("space")
    y, core = t // 2, t % 2
    x, z = s // NZ_CHIPS, s % NZ_CHIPS
    rows_dev, cells = snapshots.shape[0], snapshots.shape[1]
    out_rows, out_cells = rows_dev // 2, cells // 2
    half = out_rows * out_cells // 2
    chunks = rows_dev // CHUNK
    own_rows = half // NY_CHIPS

    take_mask = pltpu.make_async_copy(mask, mask_own.at[pl.ds(0, rows_dev)], local_sem.at[1])
    take_mask.start()
    take_taps = [
        pltpu.make_async_copy(taps_rows, row_taps, local_sem.at[2]),
        pltpu.make_async_copy(taps_cols, col_taps, local_sem.at[3]),
    ]
    for taps in take_taps:
        taps.start()

    chunk_copies = [
        pltpu.make_async_copy(
            snapshots.at[pl.ds(k * CHUNK, CHUNK)], field.at[pl.ds(MARGIN + k * CHUNK, CHUNK)], chunk_sem.at[k]
        )
        for k in range(chunks)
    ]
    for copy in chunk_copies:
        copy.start()

    def at(d_z=0, d_x=0, d_y=0, flip=0):
        c = (core + flip) % 2
        return {
            "tm": ((y + d_y) % NY_CHIPS) * 2 + c,
            "space": ((x + d_x) % NX_CHIPS) * NZ_CHIPS + (z + d_z) % NZ_CHIPS,
        }

    z_offsets = range(1, NZ_CHIPS)
    x_offsets = range(1, NX_CHIPS)
    y_offsets = range(1, NY_CHIPS)
    s_above, s_below = (s + SPACE - 1) % SPACE, (s + 1) % SPACE
    barrier = pltpu.get_barrier_semaphore()
    xy_offsets = [(a, b) for a in range(NX_CHIPS) for b in range(NY_CHIPS) if a or b]
    peers = [at(d_z=d) for d in z_offsets] + [at(d_x=a, d_y=b) for a, b in xy_offsets]
    peers += [at(d_y=d, flip=1) for d in range(NY_CHIPS)]
    peers += [{"tm": 2 * y + c, "space": there} for c in range(2) for there in (s_above, s_below)]
    for peer in peers:
        pl.semaphore_signal(barrier, inc=1, device_id=peer, device_id_type=MESH)

    count = [0]
    unsent = []

    class Group:
        def __init__(self, landed):
            self.index, self.landed = count[0], landed
            count[0] += 1
            unsent.append(self)

        def make(self, src, dst, to):
            return pltpu.make_async_remote_copy(
                src_ref=src, dst_ref=dst, send_sem=send.at[self.index], recv_sem=recv.at[self.index],
                device_id=to, device_id_type=MESH,
            )

        def push(self, src, dst, to):
            self.make(src, dst, to).start()
            return self

        def arrive(self):
            self.make(self.landed, self.landed, at(flip=1)).wait_recv()

        def wait_send(self):
            self.make(self.landed, self.landed, at(flip=1)).wait_send()

    def push(src, dst, to, landed):
        return Group(landed).push(src, dst, to)

    take_probes = pltpu.make_async_copy(
        probes.at[rows_at(core * half + y * own_rows, own_rows)], probe_rows, local_sem.at[0]
    )
    take_probes.start()
    for margin in (0, MARGIN + rows_dev):
        field[pl.ds(margin, MARGIN)] = jnp.zeros((MARGIN, cells, COLS), jnp.float32)
    mask_own[rows_dev:, :] = jnp.zeros((COLS - rows_dev, cells), jnp.int32)
    tall[:, :EDGE] = jnp.zeros((tall.shape[0], EDGE, COLS), jnp.float32)
    tall[:, EDGE + cells :] = jnp.zeros((tall.shape[0], EDGE, COLS), jnp.float32)
    take_mask.wait()
    mask_cols = mask_own[...].astype(jnp.float32).T.astype(jnp.bfloat16)

    def mask_chunk(k):
        for r in range(k * CHUNK, (k + 1) * CHUNK):
            wet = jnp.broadcast_to(mask_cols[:, r : r + 1], (cells, COLS)).astype(jnp.float32)
            field[MARGIN + r] = field[MARGIN + r] * wet

    for taps in take_taps:
        taps.wait()
    tr = [row_taps[k] for k in range(TAPS)]
    tc = [col_taps[k] for k in range(TAPS)]

    def filter_row(i, slot):
        total = tr[0] * field[2 * i + MARGIN - 2]
        for k in range(1, TAPS):
            total = total + tr[k] * field[2 * i + MARGIN - 2 + k]
        tall[slot, EDGE : EDGE + cells] = total
        out = tc[0] * tall[slot, pl.ds(EDGE - 2, out_cells, stride=2), :]
        for k in range(1, TAPS):
            out = out + tc[k] * tall[slot, pl.ds(EDGE - 2 + k, out_cells, stride=2), :]
        return out

    def filter_half(which, store):
        slots = tall.shape[0]

        def body(step, carry):
            for slot in range(slots):
                n = step * slots + slot
                store(rows_at(n * out_cells, out_cells), filter_row(which * (out_rows // 2) + n, slot))
            return carry

        lax.fori_loop(0, out_rows // 2 // slots, body, 0)

    def store_away(rows, value):
        away[rows, :] = value

    def store_own(rows, value):
        pair[core, rows, :] = value

    for copy in chunk_copies:
        copy.wait()
    for k in range(chunks):
        mask_chunk(k)
    edges[0] = filter_row(-1, 0)
    edges[1] = filter_row(out_rows, 1)
    filter_half(1 - core, store_away)
    pl.semaphore_wait(barrier, len(peers))
    crossed = push(away, pair.at[core], at(flip=1), pair.at[1 - core])
    edge_group = Group(edge_in)
    edge_group.push(edges.at[0], edge_in.at[core], {"tm": 2 * y + 1, "space": s_above})
    edge_group.push(edges.at[1], edge_in.at[core], {"tm": 2 * y, "space": s_below})
    filter_half(core, store_own)
    edge_group.arrive()
    crossed.arrive()
    touches = ((s > 0) & (core == 0)) | ((s < SPACE - 1) & (core == 1))
    edge_rows = rows_at((out_rows // 2 - 1) * out_cells * core, out_cells)
    for c in range(2):
        pair[c, edge_rows, :] = pair[c, edge_rows, :] + jnp.where(touches, edge_in[c], 0.0)

    def plane_sum(part, gath, cbuf, zbuf, xbuf):
        rows = part.shape[0] // 2
        piece = rows // NZ_CHIPS
        mine = core * rows
        push(part.at[rows_at((1 - core) * rows, rows)], cbuf, at(flip=1), cbuf).arrive()
        part[rows_at(mine, rows), :] = part[rows_at(mine, rows), :] + cbuf[...]
        group = Group(zbuf)
        for d in z_offsets:
            group.push(part.at[rows_at(mine + (z + d) % NZ_CHIPS * piece, piece)], zbuf.at[d - 1], at(d_z=d))
        group.arrive()
        total = part[rows_at(mine + z * piece, piece), :]
        for d in z_offsets:
            total = total + zbuf[d - 1]
        xbuf[x] = total
        group = Group(xbuf.at[pl.ds(0, NX_CHIPS - 1)])
        for d in x_offsets:
            group.push(xbuf.at[x], xbuf.at[x], at(d_x=d))
        group.arrive()
        own = gath.at[rows_at(mine + z * piece, piece)]
        gath[rows_at(mine + z * piece, piece), :] = (xbuf[0] + xbuf[1]) + (xbuf[2] + xbuf[3])
        group = Group(gath.at[rows_at(mine, (NZ_CHIPS - 1) * piece)])
        for d in z_offsets:
            group.push(own, own, at(d_z=d))
        group.arrive()
        ours, theirs = gath.at[rows_at(mine, rows)], gath.at[rows_at((1 - core) * rows, rows)]
        push(ours, ours, at(flip=1), theirs).arrive()

    class WholeSum:
        def __init__(self, part, gath, cbuf, rbuf, zbuf):
            self.part, self.gath, self.cbuf, self.rbuf, self.zbuf = part, gath, cbuf, rbuf, zbuf
            self.rows = part.shape[0] // 2
            self.piece = self.rows // XY_CHIPS
            self.ours = rows_at(core * self.rows, self.rows)
            self.theirs = rows_at((1 - core) * self.rows, self.rows)

        def piece_of(self, a, b):
            owner = (x + a) % NX_CHIPS * NY_CHIPS + (y + b) % NY_CHIPS
            return rows_at(core * self.rows + owner * self.piece, self.piece)

        def start(self):
            self.came = push(self.part.at[self.theirs], self.cbuf, at(flip=1), self.cbuf)

        def scatter(self):
            self.came.arrive()
            self.part[self.ours, :] = self.part[self.ours, :] + self.cbuf[...]
            self.came = Group(self.rbuf)
            for n, (a, b) in enumerate(xy_offsets):
                self.came.push(self.part.at[self.piece_of(a, b)], self.rbuf.at[n], at(d_x=a, d_y=b))

        def along_z(self):
            self.came.arrive()
            total = self.part[self.piece_of(0, 0), :]
            for n in range(len(xy_offsets)):
                total = total + self.rbuf[n]
            self.zbuf[z] = total
            self.came = Group(self.zbuf.at[pl.ds(0, NZ_CHIPS - 1)])
            for d in z_offsets:
                self.came.push(self.zbuf.at[z], self.zbuf.at[z], at(d_z=d))

        def gather(self):
            self.came.arrive()
            terms = [self.zbuf[k] for k in range(NZ_CHIPS)]
            while len(terms) > 1:
                terms = [terms[k] + terms[k + 1] for k in range(0, len(terms), 2)]
            own = self.piece_of(0, 0)
            self.gath[own, :] = terms[0]
            own = self.gath.at[own]
            self.came = Group(self.gath.at[rows_at(core * self.rows, (XY_CHIPS - 1) * self.piece)])
            for a, b in xy_offsets:
                self.came.push(own, own, at(d_x=a, d_y=b))

        def share(self):
            self.came.arrive()
            ours, theirs = self.gath.at[self.ours], self.gath.at[self.theirs]
            self.came = push(ours, ours, at(flip=1), theirs)

        def finish(self):
            self.came.arrive()

    gram[...] = jnp.zeros_like(gram)

    def add_rows(chunk, carry):
        rows = rows_at(chunk * own_rows, own_rows)
        high, low = halves(jnp.concatenate([pair[0, rows, :], pair[1, rows, :]], axis=1))
        cat_high[rows, :] = high
        cat_low[rows, :] = low
        cross = dot(high, low, TN)
        gram[...] = gram[...] + (dot(high, high, TN) + (cross + cross.T))
        return carry

    lax.fori_loop(0, NY_CHIPS, add_rows, 0)
    part1[:COLS] = gram[:COLS, :COLS]
    part1[COLS : 2 * COLS] = gram[:COLS, COLS:]
    part1[2 * COLS :] = gram[COLS:, COLS:]
    plane_sum(part1, gath1, cbuf1, zbuf1, xbuf1)
    total = block_2x2(gath1[:COLS], gath1[COLS : 2 * COLS], gath1[2 * COLS :])
    start_sign(total, sign.at[0])
    run_signs(SIGN_STEPS, sign.at[0])
    combine = combine_of(sign.at[0])
    combine_halves = halves(combine)

    quarters = Group(rows4.at[pl.ds(0, NY_CHIPS - 1)])
    for d in [2, 1, 3, 0]:
        to = (y + d) % NY_CHIPS
        rows = rows_at(to * own_rows, own_rows)
        merged = dot3((cat_high[rows, :], cat_low[rows, :]), combine_halves)
        if d:
            quarter[d - 1] = merged
            quarters.push(quarter.at[d - 1], rows4.at[y], at(d_y=d))
        else:
            rows4[y] = merged
    diag[y] = mul(combine, mul(total, combine), TN)
    diags = Group(diag.at[pl.ds(0, NY_CHIPS - 1)])
    for d in y_offsets:
        diags.push(diag.at[y], diag.at[y], at(d_y=d))
    take_probes.wait()
    quarters.arrive()

    f4 = [halves(rows4[p]) for p in range(NY_CHIPS)]
    probe_halves = halves(probe_rows[...])
    sum_now = WholeSum(part2, gath2, cbuf2, rbuf2, zbuf2)
    sum_later = WholeSum(part3, gath3, cbuf3, rbuf3, zbuf3)

    def beside(*blocks):
        return tuple(jnp.concatenate([block[h] for block in blocks], axis=1) for h in range(2))

    products = dot3(beside(f4[0], f4[2]), beside(f4[1], f4[3]), TN)
    part2[:COLS] = products[:COLS, :COLS]
    part2[COLS:] = products[COLS:, COLS:]
    sum_now.start()
    sum_now.scatter()
    products = dot3(beside(f4[0], f4[1]), beside(f4[2], f4[3], probe_halves), TN)
    for n, (p, q) in enumerate([(0, 0), (0, 1), (1, 0), (1, 1), (0, 2), (1, 2)]):
        part3[n * COLS : (n + 1) * COLS] = products[p * COLS : (p + 1) * COLS, q * COLS : (q + 1) * COLS]
    part3[6 * COLS :] = dot3(beside(f4[2], f4[3]), probe_halves, TN)
    sum_later.start()
    sum_later.scatter()
    sum_now.along_z()
    sum_later.along_z()
    sum_now.gather()
    sum_later.gather()
    sum_now.share()
    diags.arrive()
    sum_now.finish()

    def summed(index):
        return gath3[index * COLS : (index + 1) * COLS]

    def gram_of(which):
        return block_2x2(diag[2 * which], gath2[rows_at(which * COLS, COLS), :], diag[2 * which + 1])

    def diag_of(which):
        c = halves(combines[which])
        return dot3(c, halves(dot3(halves(gram_of(which)), c)), TN)

    start_sign(gram_of(core), sign.at[0])
    run_signs(6, sign.at[0])
    sum_later.share()
    run_signs(SIGN_STEPS - 6, sign.at[0])
    combines[core] = combine_of(sign.at[0])
    swapped = push(combines.at[core], combines.at[core], at(flip=1), combines.at[1 - core])
    diag_next[core] = diag_of(core)
    sum_later.finish()
    swapped.arrive()
    diag_next[1 - core] = diag_of(1 - core)
    low_h, high_h = halves(combines[0]), halves(combines[1])
    crossing = jnp.concatenate(
        [jnp.concatenate([summed(0), summed(1)], axis=1), jnp.concatenate([summed(2), summed(3)], axis=1)], axis=0
    )
    cross = dot3(low_h, halves(dot3(halves(crossing), high_h)), TN)

    start_sign(block_2x2(diag_next[0], cross, diag_next[1]), sign.at[0])
    run_signs(SIGN_STEPS, sign.at[0])
    last = combine_of(sign.at[0])
    whole = halves(
        jnp.concatenate([dot3(low_h, halves(last[:COLS])), dot3(high_h, halves(last[COLS:]))], axis=0)
    )
    all4 = tuple(jnp.concatenate([f[h] for f in [halves(rows4[p]) for p in range(NY_CHIPS)]], axis=1) for h in range(2))
    basis = dot3(all4, whole)
    for k in range(own_rows // out_cells):
        turned[k] = basis[k * out_cells : (k + 1) * out_cells].T
    width = COLS // 8

    def grid_rows(place):
        count = own_rows // out_cells
        return pl.ds(place * count, count)

    place_own = core * NY_CHIPS + y
    outward = Group(pieces.at[pl.ds(0, out_rows - out_rows // 8)])
    for f in range(2):
        for d in range(NY_CHIPS):
            if d or f:
                to_t = ((y + d) % NY_CHIPS) * 2 + (core + f) % 2
                outward.push(
                    turned.at[:, rows_at(to_t * width, width)], pieces.at[grid_rows(place_own)], at(d_y=d, flip=f)
                )
    pieces[grid_rows(place_own)] = turned[:, rows_at(t * width, width), :]
    coef_all[...] = dot3(whole, halves(gath3[4 * COLS :]), TN)
    coef[...] = coef_all[rows_at(t * width, width), :]
    outward.arrive()
    assert count[0] == GROUPS
    for out in unsent:
        out.wait_send()


def merge_all(snapshots, mask, taps_rows, taps_cols, probes):
    rows_dev, cells, cols = snapshots.shape
    rows = rows_dev // 2 * (cells // 2)
    half = rows // 2
    own_rows = half // NY_CHIPS
    f32, vmem = jnp.float32, pltpu.VMEM
    piece1 = FIRST_ROWS // 2 // NZ_CHIPS
    piece2, piece3 = SECOND_ROWS // 2 // XY_CHIPS, LATER_ROWS // 2 // XY_CHIPS
    return pl.pallas_call(
        merge_kernel,
        out_shape=(
            pltpu.VMEM((rows_dev // 2, cols // 8, cells // 2), f32),
            pltpu.VMEM((cols // 8, cols), f32),
        ),
        in_specs=[pl.BlockSpec(memory_space=pl.ANY)] * 5,
        out_specs=(pl.BlockSpec(memory_space=pltpu.VMEM), pl.BlockSpec(memory_space=pltpu.VMEM)),
        scratch_shapes=[
            pltpu.SMEM((TAPS,), f32),
            pltpu.SMEM((TAPS,), f32),
            vmem((rows_dev + 2 * MARGIN, cells, cols), f32),
            vmem((COLS, cells), jnp.int32),
            vmem((4, cells + 2 * EDGE, cols), f32),
            vmem((2, cells // 2, cols), f32),
            vmem((2, cells // 2, cols), f32),
            vmem((half, cols), f32),
            vmem((2, half, cols), f32),
            vmem((half, 2 * cols), jnp.bfloat16),
            vmem((half, 2 * cols), jnp.bfloat16),
            vmem((2 * cols, 2 * cols), f32),
            vmem((FIRST_ROWS, cols), f32),
            vmem((FIRST_ROWS, cols), f32),
            vmem((FIRST_ROWS // 2, cols), f32),
            vmem((NZ_CHIPS - 1, piece1, cols), f32),
            vmem((NX_CHIPS, piece1, cols), f32),
            vmem((NY_CHIPS - 1, own_rows, cols), f32),
            vmem((NY_CHIPS, own_rows, cols), f32),
            vmem((NY_CHIPS, cols, cols), f32),
            vmem((SECOND_ROWS, cols), f32),
            vmem((SECOND_ROWS, cols), f32),
            vmem((SECOND_ROWS // 2, cols), f32),
            vmem((XY_CHIPS - 1, piece2, cols), f32),
            vmem((NZ_CHIPS, piece2, cols), f32),
            vmem((LATER_ROWS, cols), f32),
            vmem((LATER_ROWS, cols), f32),
            vmem((LATER_ROWS // 2, cols), f32),
            vmem((XY_CHIPS - 1, piece3, cols), f32),
            vmem((NZ_CHIPS, piece3, cols), f32),
            vmem((1, 2 * cols, 2 * cols), f32),
            vmem((own_rows, cols), f32),
            vmem((own_rows * 2 // cells, cols, cells // 2), f32),
            vmem((cols, cols), f32),
            vmem((2, 2 * cols, cols), f32),
            vmem((2, cols, cols), f32),
            pltpu.SemaphoreType.DMA((GROUPS,)),
            pltpu.SemaphoreType.DMA((GROUPS,)),
            pltpu.SemaphoreType.DMA((4,)),
            pltpu.SemaphoreType.DMA((rows_dev // CHUNK,)),
        ],
        compiler_params=pltpu.CompilerParams(
            collective_id=1, has_side_effects=True
        ),
        name="merge_all",
    )(snapshots, mask, taps_rows, taps_cols, probes)


def local(snapshots, land_mask, taps_rows, taps_cols, probes):
    rows_dev, cell_cols, columns = snapshots.shape
    cell_rows = rows_dev // 2 * (cell_cols // 2)
    flat_probes = probes.reshape(cell_rows, probes.shape[2])
    pieces, coef_own = merge_all(snapshots, land_mask, taps_rows, taps_cols, flat_probes)
    return (pieces.transpose(0, 2, 1), coef_own)


def solution(mesh):
    placed = (P("space", None, "tm"), P("space", None), P(), P(), P("space", None, None))
    return jax.shard_map(
        local,
        mesh=mesh,
        in_specs=placed,
        out_specs=(P("space", None, "tm"), P("tm", None)),
        check_vma=False,
    )
```

```python
import functools

import jax
import jax.numpy as jnp
from jax import lax
from jax.experimental import pallas as pl
from jax.experimental.pallas import tpu as pltpu
from jax.sharding import PartitionSpec as P

SIGN_STEPS = 8
GROUPS = 21
NX_CHIPS, NY_CHIPS, NZ_CHIPS = 4, 4, 8
SPACE, XY_CHIPS = NX_CHIPS * NZ_CHIPS, NX_CHIPS * NY_CHIPS
COLS = 128
FIRST_ROWS, SECOND_ROWS, LATER_ROWS = 3 * COLS, 2 * COLS, 8 * COLS
TAPS, CHUNK, EDGE, MARGIN = 6, 8, 8, 4
MESH = pl.DeviceIdType.MESH

def rows_at(start, size):
    return pl.ds(pl.multiple_of(start, 8), size)


NN = (((1,), (0,)), ((), ()))
TN = (((0,), (0,)), ((), ()))


def halves(a):
    high = a.astype(jnp.bfloat16)
    return high, (a - high.astype(jnp.float32)).astype(jnp.bfloat16)


def dot(a, b, dims):
    return lax.dot_general(a, b, dims, preferred_element_type=jnp.float32)


def dot3(a, b, dims=NN):
    (a_high, a_low), (b_high, b_low) = a, b
    (a_dim,), (b_dim,) = dims[0]
    left = jnp.concatenate([a_high, a_low, a_high], axis=a_dim)
    right = jnp.concatenate([b_high, b_high, b_low], axis=b_dim)
    return dot(left, right, dims)


def mul(a, b, dims=NN):
    return dot3(halves(a), halves(b), dims)


def block_2x2(low, cross, high):
    return jnp.concatenate(
        [jnp.concatenate([low, cross], axis=1), jnp.concatenate([cross.T, high], axis=1)], axis=0
    )


def start_sign(gram, y_ref):
    order = gram.shape[0]
    identity = lax.broadcasted_iota(jnp.int32, gram.shape, 0) == lax.broadcasted_iota(jnp.int32, gram.shape, 1)
    mean_eig = jnp.sum(jnp.where(identity, gram, 0.0), keepdims=True) / order
    shifted = gram - jnp.where(identity, mean_eig, 0.0)
    y_ref[...] = shifted / jnp.sqrt(jnp.sum(shifted * shifted, keepdims=True) + 1e-06)


def sign_step(y_ref):
    y = y_ref[...]
    y_halves = halves(y)
    square = dot3(y_halves, y_halves)
    identity = lax.broadcasted_iota(jnp.int32, y.shape, 0) == lax.broadcasted_iota(jnp.int32, y.shape, 1)
    y_ref[...] = dot3(y_halves, halves(jnp.where(identity, 1.5, 0.0) - 0.5 * square))


def combine_of(y_ref):
    y = y_ref[...]
    order = y.shape[0]
    row = lax.broadcasted_iota(jnp.int32, (order, order // 2), 0)
    col = lax.broadcasted_iota(jnp.int32, (order, order // 2), 1)
    ones = jnp.where((row == col) | (row == col + order // 2), 0.5, 0.0)
    return ones + 0.5 * (y[:, : order // 2] + y[:, order // 2 :])


def run_signs(steps, *refs):
    def body(step, carry):
        for ref in refs:
            sign_step(ref)
        return carry

    lax.fori_loop(0, steps, body, 0, unroll=2)


def merge_kernel(snapshots, mask, taps_rows, taps_cols, probes, pieces, coef,
                 row_taps, col_taps, field, mask_own, tall, edges, edge_in, away, pair, cat_high, cat_low, gram, part1, gath1, cbuf1, zbuf1, xbuf1,
                 quarter, rows4, diag, part2, gath2, cbuf2, rbuf2, zbuf2,
                 part3, gath3, cbuf3, rbuf3, zbuf3, sign, probe_rows, turned, coef_all, combines, diag_next,
                 send, recv, local_sem, chunk_sem):
    t = lax.axis_index("tm")
    s = lax.axis_index("space")
    y, core = t // 2, t % 2
    x, z = s // NZ_CHIPS, s % NZ_CHIPS
    rows_dev, cells = snapshots.shape[0], snapshots.shape[1]
    out_rows, out_cells = rows_dev // 2, cells // 2
    half = out_rows * out_cells // 2
    chunks = rows_dev // CHUNK
    own_rows = half // NY_CHIPS

    take_mask = pltpu.make_async_copy(mask, mask_own.at[pl.ds(0, rows_dev)], local_sem.at[1])
    take_mask.start()
    take_taps = [
        pltpu.make_async_copy(taps_rows, row_taps, local_sem.at[2]),
        pltpu.make_async_copy(taps_cols, col_taps, local_sem.at[3]),
    ]
    for taps in take_taps:
        taps.start()

    chunk_copies = [
        pltpu.make_async_copy(
            snapshots.at[pl.ds(k * CHUNK, CHUNK)], field.at[pl.ds(MARGIN + k * CHUNK, CHUNK)], chunk_sem.at[k]
        )
        for k in range(chunks)
    ]
    for copy in chunk_copies:
        copy.start()

    def at(d_z=0, d_x=0, d_y=0, flip=0):
        c = (core + flip) % 2
        return {
            "tm": ((y + d_y) % NY_CHIPS) * 2 + c,
            "space": ((x + d_x) % NX_CHIPS) * NZ_CHIPS + (z + d_z) % NZ_CHIPS,
        }

    z_offsets = range(1, NZ_CHIPS)
    x_offsets = range(1, NX_CHIPS)
    y_offsets = range(1, NY_CHIPS)
    s_above, s_below = (s + SPACE - 1) % SPACE, (s + 1) % SPACE
    barrier = pltpu.get_barrier_semaphore()
    xy_offsets = [(a, b) for a in range(NX_CHIPS) for b in range(NY_CHIPS) if a or b]
    peers = [at(d_z=d) for d in z_offsets] + [at(d_x=a, d_y=b) for a, b in xy_offsets]
    peers += [at(d_y=d, flip=1) for d in range(NY_CHIPS)]
    peers += [{"tm": 2 * y + c, "space": there} for c in range(2) for there in (s_above, s_below)]
    for peer in peers:
        pl.semaphore_signal(barrier, inc=1, device_id=peer, device_id_type=MESH)

    count = [0]
    unsent = []

    class Group:
        def __init__(self, landed):
            self.index, self.landed = count[0], landed
            count[0] += 1
            unsent.append(self)

        def make(self, src, dst, to):
            return pltpu.make_async_remote_copy(
                src_ref=src, dst_ref=dst, send_sem=send.at[self.index], recv_sem=recv.at[self.index],
                device_id=to, device_id_type=MESH,
            )

        def push(self, src, dst, to):
            self.make(src, dst, to).start()
            return self

        def arrive(self):
            self.make(self.landed, self.landed, at(flip=1)).wait_recv()

        def wait_send(self):
            self.make(self.landed, self.landed, at(flip=1)).wait_send()

    def push(src, dst, to, landed):
        return Group(landed).push(src, dst, to)

    take_probes = pltpu.make_async_copy(
        probes.at[rows_at(core * half + y * own_rows, own_rows)], probe_rows, local_sem.at[0]
    )
    take_probes.start()
    for margin in (0, MARGIN + rows_dev):
        field[pl.ds(margin, MARGIN)] = jnp.zeros((MARGIN, cells, COLS), jnp.float32)
    mask_own[rows_dev:, :] = jnp.zeros((COLS - rows_dev, cells), jnp.int32)
    tall[:, :EDGE] = jnp.zeros((tall.shape[0], EDGE, COLS), jnp.float32)
    tall[:, EDGE + cells :] = jnp.zeros((tall.shape[0], EDGE, COLS), jnp.float32)
    take_mask.wait()
    mask_cols = mask_own[...].astype(jnp.float32).T.astype(jnp.bfloat16)

    def mask_chunk(k):
        for r in range(k * CHUNK, (k + 1) * CHUNK):
            wet = jnp.broadcast_to(mask_cols[:, r : r + 1], (cells, COLS)).astype(jnp.float32)
            field[MARGIN + r] = field[MARGIN + r] * wet

    for taps in take_taps:
        taps.wait()
    tr = [row_taps[k] for k in range(TAPS)]
    tc = [col_taps[k] for k in range(TAPS)]

    def filter_row(i, slot):
        total = tr[0] * field[2 * i + MARGIN - 2]
        for k in range(1, TAPS):
            total = total + tr[k] * field[2 * i + MARGIN - 2 + k]
        tall[slot, EDGE : EDGE + cells] = total
        out = tc[0] * tall[slot, pl.ds(EDGE - 2, out_cells, stride=2), :]
        for k in range(1, TAPS):
            out = out + tc[k] * tall[slot, pl.ds(EDGE - 2 + k, out_cells, stride=2), :]
        return out

    def filter_half(which, store):
        slots = tall.shape[0]

        def body(step, carry):
            for slot in range(slots):
                n = step * slots + slot
                store(rows_at(n * out_cells, out_cells), filter_row(which * (out_rows // 2) + n, slot))
            return carry

        lax.fori_loop(0, out_rows // 2 // slots, body, 0)

    def store_away(rows, value):
        away[rows, :] = value

    def store_own(rows, value):
        pair[core, rows, :] = value

    for copy in chunk_copies:
        copy.wait()
    for k in range(chunks):
        mask_chunk(k)
    edges[0] = filter_row(-1, 0)
    edges[1] = filter_row(out_rows, 1)
    filter_half(1 - core, store_away)
    pl.semaphore_wait(barrier, len(peers))
    crossed = push(away, pair.at[core], at(flip=1), pair.at[1 - core])
    edge_group = Group(edge_in)
    edge_group.push(edges.at[0], edge_in.at[core], {"tm": 2 * y + 1, "space": s_above})
    edge_group.push(edges.at[1], edge_in.at[core], {"tm": 2 * y, "space": s_below})
    filter_half(core, store_own)
    edge_group.arrive()
    crossed.arrive()
    touches = ((s > 0) & (core == 0)) | ((s < SPACE - 1) & (core == 1))
    edge_rows = rows_at((out_rows // 2 - 1) * out_cells * core, out_cells)
    for c in range(2):
        pair[c, edge_rows, :] = pair[c, edge_rows, :] + jnp.where(touches, edge_in[c], 0.0)

    def plane_sum(part, gath, cbuf, zbuf, xbuf):
        rows = part.shape[0] // 2
        piece = rows // NZ_CHIPS
        mine = core * rows
        push(part.at[rows_at((1 - core) * rows, rows)], cbuf, at(flip=1), cbuf).arrive()
        part[rows_at(mine, rows), :] = part[rows_at(mine, rows), :] + cbuf[...]
        group = Group(zbuf)
        for d in z_offsets:
            group.push(part.at[rows_at(mine + (z + d) % NZ_CHIPS * piece, piece)], zbuf.at[d - 1], at(d_z=d))
        group.arrive()
        total = part[rows_at(mine + z * piece, piece), :]
        for d in z_offsets:
            total = total + zbuf[d - 1]
        xbuf[x] = total
        group = Group(xbuf.at[pl.ds(0, NX_CHIPS - 1)])
        for d in x_offsets:
            group.push(xbuf.at[x], xbuf.at[x], at(d_x=d))
        group.arrive()
        own = gath.at[rows_at(mine + z * piece, piece)]
        gath[rows_at(mine + z * piece, piece), :] = (xbuf[0] + xbuf[1]) + (xbuf[2] + xbuf[3])
        group = Group(gath.at[rows_at(mine, (NZ_CHIPS - 1) * piece)])
        for d in z_offsets:
            group.push(own, own, at(d_z=d))
        group.arrive()
        ours, theirs = gath.at[rows_at(mine, rows)], gath.at[rows_at((1 - core) * rows, rows)]
        push(ours, ours, at(flip=1), theirs).arrive()

    class WholeSum:
        def __init__(self, part, gath, cbuf, rbuf, zbuf):
            self.part, self.gath, self.cbuf, self.rbuf, self.zbuf = part, gath, cbuf, rbuf, zbuf
            self.rows = part.shape[0] // 2
            self.piece = self.rows // XY_CHIPS
            self.ours = rows_at(core * self.rows, self.rows)
            self.theirs = rows_at((1 - core) * self.rows, self.rows)

        def piece_of(self, a, b):
            owner = (x + a) % NX_CHIPS * NY_CHIPS + (y + b) % NY_CHIPS
            return rows_at(core * self.rows + owner * self.piece, self.piece)

        def start(self):
            self.came = push(self.part.at[self.theirs], self.cbuf, at(flip=1), self.cbuf)

        def scatter(self):
            self.came.arrive()
            self.part[self.ours, :] = self.part[self.ours, :] + self.cbuf[...]
            self.came = Group(self.rbuf)
            for n, (a, b) in enumerate(xy_offsets):
                self.came.push(self.part.at[self.piece_of(a, b)], self.rbuf.at[n], at(d_x=a, d_y=b))

        def along_z(self):
            self.came.arrive()
            total = self.part[self.piece_of(0, 0), :]
            for n in range(len(xy_offsets)):
                total = total + self.rbuf[n]
            self.zbuf[z] = total
            self.came = Group(self.zbuf.at[pl.ds(0, NZ_CHIPS - 1)])
            for d in z_offsets:
                self.came.push(self.zbuf.at[z], self.zbuf.at[z], at(d_z=d))

        def gather(self):
            self.came.arrive()
            terms = [self.zbuf[k] for k in range(NZ_CHIPS)]
            while len(terms) > 1:
                terms = [terms[k] + terms[k + 1] for k in range(0, len(terms), 2)]
            own = self.piece_of(0, 0)
            self.gath[own, :] = terms[0]
            own = self.gath.at[own]
            self.came = Group(self.gath.at[rows_at(core * self.rows, (XY_CHIPS - 1) * self.piece)])
            for a, b in xy_offsets:
                self.came.push(own, own, at(d_x=a, d_y=b))

        def share(self):
            self.came.arrive()
            ours, theirs = self.gath.at[self.ours], self.gath.at[self.theirs]
            self.came = push(ours, ours, at(flip=1), theirs)

        def finish(self):
            self.came.arrive()

    gram[...] = jnp.zeros_like(gram)

    def add_rows(chunk, carry):
        rows = rows_at(chunk * own_rows, own_rows)
        high, low = halves(jnp.concatenate([pair[0, rows, :], pair[1, rows, :]], axis=1))
        cat_high[rows, :] = high
        cat_low[rows, :] = low
        cross = dot(high, low, TN)
        gram[...] = gram[...] + (dot(high, high, TN) + (cross + cross.T))
        return carry

    lax.fori_loop(0, NY_CHIPS, add_rows, 0)
    part1[:COLS] = gram[:COLS, :COLS]
    part1[COLS : 2 * COLS] = gram[:COLS, COLS:]
    part1[2 * COLS :] = gram[COLS:, COLS:]
    plane_sum(part1, gath1, cbuf1, zbuf1, xbuf1)
    total = block_2x2(gath1[:COLS], gath1[COLS : 2 * COLS], gath1[2 * COLS :])
    start_sign(total, sign.at[0])
    run_signs(SIGN_STEPS, sign.at[0])
    combine = combine_of(sign.at[0])
    combine_halves = halves(combine)

    quarters = Group(rows4.at[pl.ds(0, NY_CHIPS - 1)])
    for d in [2, 1, 3, 0]:
        to = (y + d) % NY_CHIPS
        rows = rows_at(to * own_rows, own_rows)
        merged = dot3((cat_high[rows, :], cat_low[rows, :]), combine_halves)
        if d:
            quarter[d - 1] = merged
            quarters.push(quarter.at[d - 1], rows4.at[y], at(d_y=d))
        else:
            rows4[y] = merged
    diag[y] = mul(combine, mul(total, combine), TN)
    diags = Group(diag.at[pl.ds(0, NY_CHIPS - 1)])
    for d in y_offsets:
        diags.push(diag.at[y], diag.at[y], at(d_y=d))
    take_probes.wait()
    quarters.arrive()

    f4 = [halves(rows4[p]) for p in range(NY_CHIPS)]
    probe_halves = halves(probe_rows[...])
    sum_now = WholeSum(part2, gath2, cbuf2, rbuf2, zbuf2)
    sum_later = WholeSum(part3, gath3, cbuf3, rbuf3, zbuf3)

    def beside(*blocks):
        return tuple(jnp.concatenate([block[h] for block in blocks], axis=1) for h in range(2))

    products = dot3(beside(f4[0], f4[2]), beside(f4[1], f4[3]), TN)
    part2[:COLS] = products[:COLS, :COLS]
    part2[COLS:] = products[COLS:, COLS:]
    sum_now.start()
    sum_now.scatter()
    products = dot3(beside(f4[0], f4[1]), beside(f4[2], f4[3], probe_halves), TN)
    for n, (p, q) in enumerate([(0, 0), (0, 1), (1, 0), (1, 1), (0, 2), (1, 2)]):
        part3[n * COLS : (n + 1) * COLS] = products[p * COLS : (p + 1) * COLS, q * COLS : (q + 1) * COLS]
    part3[6 * COLS :] = dot3(beside(f4[2], f4[3]), probe_halves, TN)
    sum_later.start()
    sum_later.scatter()
    sum_now.along_z()
    sum_later.along_z()
    sum_now.gather()
    sum_later.gather()
    sum_now.share()
    diags.arrive()
    sum_now.finish()

    def summed(index):
        return gath3[index * COLS : (index + 1) * COLS]

    def gram_of(which):
        return block_2x2(diag[2 * which], gath2[rows_at(which * COLS, COLS), :], diag[2 * which + 1])

    def diag_of(which):
        c = halves(combines[which])
        return dot3(c, halves(dot3(halves(gram_of(which)), c)), TN)

    start_sign(gram_of(core), sign.at[0])
    run_signs(6, sign.at[0])
    sum_later.share()
    run_signs(SIGN_STEPS - 6, sign.at[0])
    combines[core] = combine_of(sign.at[0])
    swapped = push(combines.at[core], combines.at[core], at(flip=1), combines.at[1 - core])
    diag_next[core] = diag_of(core)
    sum_later.finish()
    swapped.arrive()
    diag_next[1 - core] = diag_of(1 - core)
    low_h, high_h = halves(combines[0]), halves(combines[1])
    crossing = jnp.concatenate(
        [jnp.concatenate([summed(0), summed(1)], axis=1), jnp.concatenate([summed(2), summed(3)], axis=1)], axis=0
    )
    cross = dot3(low_h, halves(dot3(halves(crossing), high_h)), TN)

    start_sign(block_2x2(diag_next[0], cross, diag_next[1]), sign.at[0])
    run_signs(SIGN_STEPS, sign.at[0])
    last = combine_of(sign.at[0])
    whole = halves(
        jnp.concatenate([dot3(low_h, halves(last[:COLS])), dot3(high_h, halves(last[COLS:]))], axis=0)
    )
    all4 = beside(*f4)
    basis = dot3(all4, whole)
    for k in range(own_rows // out_cells):
        turned[k] = basis[k * out_cells : (k + 1) * out_cells].T
    width = COLS // 8

    def grid_rows(place):
        count = own_rows // out_cells
        return pl.ds(place * count, count)

    place_own = core * NY_CHIPS + y
    outward = Group(pieces.at[pl.ds(0, out_rows - out_rows // 8)])
    for f in range(2):
        for d in range(NY_CHIPS):
            if d or f:
                to_t = ((y + d) % NY_CHIPS) * 2 + (core + f) % 2
                outward.push(
                    turned.at[:, rows_at(to_t * width, width)], pieces.at[grid_rows(place_own)], at(d_y=d, flip=f)
                )
    pieces[grid_rows(place_own)] = turned[:, rows_at(t * width, width), :]
    coef_all[...] = dot3(whole, halves(gath3[4 * COLS :]), TN)
    coef[...] = coef_all[rows_at(t * width, width), :]
    outward.arrive()
    assert count[0] == GROUPS
    for out in unsent:
        out.wait_send()


def merge_all(snapshots, mask, taps_rows, taps_cols, probes):
    rows_dev, cells, cols = snapshots.shape
    rows = rows_dev // 2 * (cells // 2)
    half = rows // 2
    own_rows = half // NY_CHIPS
    f32, vmem = jnp.float32, pltpu.VMEM
    piece1 = FIRST_ROWS // 2 // NZ_CHIPS
    piece2, piece3 = SECOND_ROWS // 2 // XY_CHIPS, LATER_ROWS // 2 // XY_CHIPS
    return pl.pallas_call(
        merge_kernel,
        out_shape=(
            pltpu.VMEM((rows_dev // 2, cols // 8, cells // 2), f32),
            pltpu.VMEM((cols // 8, cols), f32),
        ),
        in_specs=[pl.BlockSpec(memory_space=pl.ANY)] * 5,
        out_specs=(pl.BlockSpec(memory_space=pltpu.VMEM), pl.BlockSpec(memory_space=pltpu.VMEM)),
        scratch_shapes=[
            pltpu.SMEM((TAPS,), f32),
            pltpu.SMEM((TAPS,), f32),
            vmem((rows_dev + 2 * MARGIN, cells, cols), f32),
            vmem((COLS, cells), jnp.int32),
            vmem((4, cells + 2 * EDGE, cols), f32),
            vmem((2, cells // 2, cols), f32),
            vmem((2, cells // 2, cols), f32),
            vmem((half, cols), f32),
            vmem((2, half, cols), f32),
            vmem((half, 2 * cols), jnp.bfloat16),
            vmem((half, 2 * cols), jnp.bfloat16),
            vmem((2 * cols, 2 * cols), f32),
            vmem((FIRST_ROWS, cols), f32),
            vmem((FIRST_ROWS, cols), f32),
            vmem((FIRST_ROWS // 2, cols), f32),
            vmem((NZ_CHIPS - 1, piece1, cols), f32),
            vmem((NX_CHIPS, piece1, cols), f32),
            vmem((NY_CHIPS - 1, own_rows, cols), f32),
            vmem((NY_CHIPS, own_rows, cols), f32),
            vmem((NY_CHIPS, cols, cols), f32),
            vmem((SECOND_ROWS, cols), f32),
            vmem((SECOND_ROWS, cols), f32),
            vmem((SECOND_ROWS // 2, cols), f32),
            vmem((XY_CHIPS - 1, piece2, cols), f32),
            vmem((NZ_CHIPS, piece2, cols), f32),
            vmem((LATER_ROWS, cols), f32),
            vmem((LATER_ROWS, cols), f32),
            vmem((LATER_ROWS // 2, cols), f32),
            vmem((XY_CHIPS - 1, piece3, cols), f32),
            vmem((NZ_CHIPS, piece3, cols), f32),
            vmem((1, 2 * cols, 2 * cols), f32),
            vmem((own_rows, cols), f32),
            vmem((own_rows * 2 // cells, cols, cells // 2), f32),
            vmem((cols, cols), f32),
            vmem((2, 2 * cols, cols), f32),
            vmem((2, cols, cols), f32),
            pltpu.SemaphoreType.DMA((GROUPS,)),
            pltpu.SemaphoreType.DMA((GROUPS,)),
            pltpu.SemaphoreType.DMA((4,)),
            pltpu.SemaphoreType.DMA((rows_dev // CHUNK,)),
        ],
        compiler_params=pltpu.CompilerParams(
            collective_id=1, has_side_effects=True
        ),
        name="merge_all",
    )(snapshots, mask, taps_rows, taps_cols, probes)


def local(snapshots, land_mask, taps_rows, taps_cols, probes):
    rows_dev, cell_cols, columns = snapshots.shape
    cell_rows = rows_dev // 2 * (cell_cols // 2)
    flat_probes = probes.reshape(cell_rows, probes.shape[2])
    pieces, coef_own = merge_all(snapshots, land_mask, taps_rows, taps_cols, flat_probes)
    return (pieces.transpose(0, 2, 1), coef_own)


def solution(mesh):
    placed = (P("space", None, "tm"), P("space", None), P(), P(), P("space", None, None))
    return jax.shard_map(
        local,
        mesh=mesh,
        in_specs=placed,
        out_specs=(P("space", None, "tm"), P("tm", None)),
        check_vma=False,
    )
```
